256 devices in a mesh: atoms: 16 (over x, y), cols: 16 (over z, core).
Axes of the slice: x: 4, y: 4, z: 8, core: 2. Of those that a mesh axis runs over, the one named last changes fastest.
Arguments:
- supports: bfloat16 [256, 4, 27, 16, 256], P('atoms', None, None, 'cols'), may hold values from -0.012 to 0.012
- potential: bfloat16 [256, 27, 16, 256], P('atoms', None, 'cols'), may hold values from 0.1 to 4.5
- anchors: int32 [256, 3], replicated, may hold values from 0 to 47, as said below
- kernel: float32 [1024, 1024], P('atoms', 'cols'), may hold values from -0.04 to 1.1
Outputs:
- metric: float32 [1024, 1024], P('atoms', 'cols')
- hamiltonian: float32 [1024, 1024], P('atoms', 'cols')
- purified: float32 [1024, 1024], P('atoms', 'cols')
The draws below stay inside these ranges and needn't reach their ends.
Inputs may be any that keep to these rules, and one draw needn't show every extreme that they name: `anchors`: the first component of atom a's anchor lies in 3 (a // 16) to 3 (a // 16) + 2, the second and third in 0 to 3.
All inputs are finite; a program needn't handle non-finite values.
Results may differ from the reference program's by a relative error of at most 0.0003.
Values may be sent and summed in bfloat16 or wider, within the bound.
A program may use at most 128 MiB of HBM per device.

```python
import jax
import jax.numpy as jnp
from jax import lax

SLAB_ATOMS = 16
SUPPORTS = 4
BLOCK = 16
BLOCKS = 27
PURIFY_STEPS = 2
SLABS = 16
TOTAL_ATOMS = 256
FUNCTIONS = 1024


def anchor_table(key):
    base = jax.random.fold_in(key, 17)
    key_x = jax.random.fold_in(base, 1)
    key_y = jax.random.fold_in(base, 2)
    key_z = jax.random.fold_in(base, 3)
    atom_ids = jnp.arange(TOTAL_ATOMS, dtype=jnp.int32)
    slab_of = atom_ids // SLAB_ATOMS
    within = atom_ids % SLAB_ATOMS
    x_offset = jax.random.randint(key_x, (TOTAL_ATOMS,), 0, 3, dtype=jnp.int32)
    y_anchor = jax.random.randint(key_y, (TOTAL_ATOMS,), 0, 4, dtype=jnp.int32)
    z_anchor = jax.random.randint(key_z, (TOTAL_ATOMS,), 0, 4, dtype=jnp.int32)
    slab_first = within == 0
    slab_last = within == SLAB_ATOMS - 1
    last_atom = atom_ids == TOTAL_ATOMS - 1
    x_offset = jnp.where(slab_first, 0, jnp.where(slab_last, 2, x_offset))
    y_anchor = jnp.where(slab_first, 0, jnp.where(last_atom, 3, jnp.where(slab_last, 1, y_anchor)))
    z_anchor = jnp.where(slab_first, 0, jnp.where(last_atom, 3, jnp.where(slab_last, 1, z_anchor)))
    return jnp.stack([3 * slab_of + x_offset, y_anchor, z_anchor], axis=1).astype(jnp.int32)


def draw_anchors(key, part):
    return anchor_table(key)


def draw_supports(key, part):
    anchors = anchor_table(key)
    key_field = jax.random.fold_in(key, 23)
    key_noise = jax.random.fold_in(key, 29)
    key_sign = jax.random.fold_in(key, 53)
    x_blocks = 3 * SLABS + 2
    field_shape = (SUPPORTS, x_blocks * 36, BLOCK, BLOCK * BLOCK)
    own_shape = (TOTAL_ATOMS, SUPPORTS, BLOCKS, BLOCK, BLOCK * BLOCK)
    common_field = jnp.clip(jax.random.normal(key_field, field_shape, jnp.float32), -3.5, 3.5)
    own_noise = jnp.clip(jax.random.normal(key_noise, own_shape, jnp.float32), -3.5, 3.5)
    signs = 2.0 * jax.random.randint(key_sign, (TOTAL_ATOMS, SUPPORTS, 1, 1, 1), 0, 2).astype(jnp.float32) - 1.0
    block_ids = jnp.arange(BLOCKS, dtype=jnp.int32)
    block_x = block_ids // 9
    block_y = block_ids // 3 % 3
    block_z = block_ids % 3
    block_index = (anchors[:, 0:1] + block_x[None, :]) * 36 + (anchors[:, 1:2] + block_y[None, :]) * 6 + (anchors[:, 2:3] + block_z[None, :])
    common_part = jnp.take(common_field, block_index, axis=1).transpose(1, 0, 2, 3, 4)
    return (0.0015 * (common_part + own_noise) + 0.0008 * signs).astype(jnp.bfloat16)


def draw_potential(key, part):
    key_level = jax.random.fold_in(key, 31)
    key_rough = jax.random.fold_in(key, 37)
    levels = jnp.exp(jax.random.uniform(key_level, (TOTAL_ATOMS, BLOCKS, 1, 1), jnp.float32, -1.609, 1.0986))
    roughness = 1.0 + 0.5 * jax.random.uniform(key_rough, (TOTAL_ATOMS, BLOCKS, BLOCK, BLOCK * BLOCK), jnp.float32, -1.0, 1.0)
    return (levels * roughness).astype(jnp.bfloat16)


def draw_kernel(key, part):
    key_diag = jax.random.fold_in(key, 41)
    key_off = jax.random.fold_in(key, 43)
    diagonal = jax.random.uniform(key_diag, (FUNCTIONS,), jnp.float32, 0.5, 1.1)
    spread_part = 0.01 * jnp.clip(jax.random.normal(key_off, (FUNCTIONS, FUNCTIONS), jnp.float32), -4.0, 4.0)
    row_ids = jnp.arange(FUNCTIONS, dtype=jnp.int32)[:, None]
    col_ids = jnp.arange(FUNCTIONS, dtype=jnp.int32)[None, :]
    return jnp.where(row_ids == col_ids, diagonal[:, None], spread_part).astype(jnp.float32)


def setup_inputs(seed: int = 0) -> dict:
    key_list = jax.random.split(jax.random.key(seed), 5)
    supports = draw_supports(jax.random.fold_in(key_list[4], 71), 0)
    potential = draw_potential(jax.random.fold_in(key_list[4], 71), 0)
    anchors = draw_anchors(jax.random.fold_in(key_list[4], 71), 0)
    kernel = draw_kernel(jax.random.fold_in(key_list[4], 71), 0)
    return dict(supports=supports, potential=potential, anchors=anchors, kernel=kernel)


def box_layout(values):
    atom_count, func_count = values.shape[0], values.shape[1]
    box_grid = values.reshape(atom_count, func_count, 3, 3, 3, BLOCK, BLOCK, BLOCK).transpose(0, 1, 2, 5, 3, 6, 4, 7)
    return box_grid.reshape(atom_count, func_count, 3 * BLOCK, 3 * BLOCK, 3 * BLOCK)


def block_layout(box_grid):
    atom_count, func_count = box_grid.shape[0], box_grid.shape[1]
    blocked = box_grid.reshape(atom_count, func_count, 3, BLOCK, 3, BLOCK, 3, BLOCK).transpose(0, 1, 2, 4, 6, 3, 5, 7)
    return blocked.reshape(atom_count, func_count, BLOCKS, BLOCK, BLOCK * BLOCK)


def laplacian(box_grid):
    padded = jnp.pad(box_grid, ((0, 0), (0, 0), (1, 1), (1, 1), (1, 1)))
    beside = padded[:, :, 2:, 1:-1, 1:-1] + padded[:, :, :-2, 1:-1, 1:-1]
    beside = beside + padded[:, :, 1:-1, 2:, 1:-1] + padded[:, :, 1:-1, :-2, 1:-1]
    beside = beside + padded[:, :, 1:-1, 1:-1, 2:] + padded[:, :, 1:-1, 1:-1, :-2]
    return beside - 6.0 * box_grid


def pair_index(anchor_rows, anchor_band):
    offsets = anchor_band[None, :, :] - anchor_rows[:, None, :]
    block_ids = jnp.arange(27, dtype=jnp.int32)
    corner = jnp.stack([block_ids // 9, (block_ids // 3) % 3, block_ids % 3], axis=-1)
    target = corner[None, None, :, :] - offsets[:, :, None, :]
    inside = jnp.all((target >= 0) & (target <= 2), axis=-1)
    flat_index = target[..., 0] * 9 + target[..., 1] * 3 + target[..., 2]
    band_size = anchor_band.shape[0]
    slot_index = jnp.arange(band_size, dtype=jnp.int32)[None, :, None] * 27 + flat_index
    return jnp.where(inside, slot_index, band_size * 27).astype(jnp.int32)


def pair_mask(anchor_rows, anchor_cols, repeats):
    near_pair = jnp.all(jnp.abs(anchor_cols[None, :, :] - anchor_rows[:, None, :]) <= 2, axis=-1).astype(jnp.float32)
    row_atoms, col_atoms = near_pair.shape
    spread = jnp.broadcast_to(near_pair[:, None, :, None], (row_atoms, repeats, col_atoms, repeats))
    return spread.reshape(row_atoms * repeats, col_atoms * repeats)


def reference(supports, potential, anchors, kernel):
    values = supports.astype(jnp.float32)
    lap_terms = block_layout(laplacian(box_layout(values)))
    hphi = (-0.5 * lap_terms + potential.astype(jnp.float32)[:, None] * values).astype(jnp.bfloat16)
    stacked_all = jnp.concatenate([supports, hphi], axis=1)
    blank_atoms = jnp.zeros((SLAB_ATOMS,) + supports.shape[1:], jnp.bfloat16)
    padded_boxes = jnp.concatenate([blank_atoms, supports, blank_atoms], axis=0)
    far_anchor = jnp.full((SLAB_ATOMS, 3), -100, jnp.int32)
    padded_anchors = jnp.concatenate([far_anchor, anchors, far_anchor], axis=0)
    points = BLOCK * BLOCK * BLOCK
    row_count = SLAB_ATOMS * SUPPORTS

    def slab_terms(slab_index):
        start_atom = slab_index * SLAB_ATOMS
        stacked = lax.dynamic_slice_in_dim(stacked_all, start_atom, SLAB_ATOMS, 0).reshape(SLAB_ATOMS, 2 * SUPPORTS, BLOCKS, points)
        band_boxes = lax.dynamic_slice_in_dim(padded_boxes, start_atom, 3 * SLAB_ATOMS, 0)
        band_rows = band_boxes.transpose(0, 2, 1, 3, 4).reshape(3 * SLAB_ATOMS * BLOCKS, SUPPORTS * points)
        band_rows = jnp.concatenate([band_rows, jnp.zeros((1, SUPPORTS * points), jnp.bfloat16)], axis=0)
        anchor_rows = lax.dynamic_slice_in_dim(anchors, start_atom, SLAB_ATOMS, 0)
        anchor_band = lax.dynamic_slice_in_dim(padded_anchors, start_atom, 3 * SLAB_ATOMS, 0)
        lookup = pair_index(anchor_rows, anchor_band)

        def atom_terms(pieces):
            stacked_row, lookup_row = pieces
            picked = jnp.take(band_rows, lookup_row.reshape(-1), axis=0).reshape(3 * SLAB_ATOMS, BLOCKS, SUPPORTS, points)
            return jnp.einsum("hpx,bpgx->hbg", stacked_row.astype(jnp.float32), picked.astype(jnp.float32))

        gram_terms = lax.map(atom_terms, (stacked, lookup))
        gram_terms = gram_terms.reshape(SLAB_ATOMS, 2, SUPPORTS, 3 * SLAB_ATOMS, SUPPORTS).transpose(1, 0, 2, 3, 4)
        return gram_terms.reshape(2, row_count, 3 * row_count)

    band_blocks = lax.map(slab_terms, jnp.arange(SLABS, dtype=jnp.int32))
    widened = jnp.zeros((2, FUNCTIONS, FUNCTIONS + 2 * row_count), jnp.float32)
    for slab_index in range(SLABS):
        widened = widened.at[:, slab_index * row_count:(slab_index + 1) * row_count, slab_index * row_count:slab_index * row_count + 3 * row_count].set(band_blocks[slab_index])
    matrices = widened[:, :, row_count:row_count + FUNCTIONS]
    metric = matrices[0]
    hamiltonian = matrices[1]
    truncation = pair_mask(anchors, anchors, SUPPORTS)
    purified = kernel
    for iteration in range(PURIFY_STEPS):
        product_one = jnp.dot(purified, metric, precision=lax.Precision.HIGHEST, preferred_element_type=jnp.float32)
        product_two = jnp.dot(product_one, purified, precision=lax.Precision.HIGHEST, preferred_element_type=jnp.float32)
        product_three = jnp.dot(product_one, product_two, precision=lax.Precision.HIGHEST, preferred_element_type=jnp.float32)
        purified = truncation * (3.0 * product_two - 2.0 * product_three)
    return metric, hamiltonian, purified
```

```python
import functools

import jax
import jax.numpy as jnp
from jax import lax
from jax.experimental import pallas as pl
from jax.experimental.pallas import tpu as pltpu
from jax.sharding import PartitionSpec as P

MESH = pl.DeviceIdType.MESH
F32 = jnp.float32
BF16 = jnp.bfloat16
GRID_BLOCKS = 180
ATOMS = 16
FUNCS = 4
ROWS = ATOMS * FUNCS


def split(a):
    high = a.astype(BF16)
    return high, (a - high.astype(F32)).astype(BF16)


def dot3(left, right, dims=(((1,), (0,)), ((), ()))):
    lh, ll = left
    rh, rl = right
    mm = functools.partial(lax.dot_general, dimension_numbers=dims, preferred_element_type=F32)
    return mm(lh, rh) + (mm(lh, rl) + mm(ll, rh))


def shift_matrices():
    source = lax.broadcasted_iota(jnp.int32, (256, 256), 0)
    target = lax.broadcasted_iota(jnp.int32, (256, 256), 1)
    step = target - source
    z = target % 16
    one = jnp.float32(1.0)
    own = jnp.where(step == 0, -6.0, 0.0)
    own = own + jnp.where((step == 1) & (z != 0), one, 0.0)
    own = own + jnp.where((step == -1) & (z != 15), one, 0.0)
    own = own + jnp.where((step == 16) | (step == -16), one, 0.0)
    z_low = jnp.where((step == -15) & (z == 0), one, 0.0)
    z_high = jnp.where((step == 15) & (z == 15), one, 0.0)
    y_low = jnp.where(step == -240, one, 0.0)
    y_high = jnp.where(step == 240, one, 0.0)
    return [m.astype(BF16) for m in (own, z_low, z_high, y_low, y_high)]


def mm(a, b):
    return jnp.dot(a, b, preferred_element_type=F32)


def gram_kernel(sc, x_ref, lo_ref, hi_ref, bl_ref, bu_ref, v_ref, out_ref, grid, lap):
    def clear(g, carry):
        grid[g] = jnp.zeros((3 * ROWS, 256), BF16)
        return carry

    lax.fori_loop(0, GRID_BLOCKS + 1, clear, 0)
    own, z_low, z_high, y_low, y_high = shift_matrices()
    for bx in range(3):
        base = 9 * bx
        rows = lambda first, count: x_ref[base + first : base + first + count].reshape(count * ROWS, 256)
        lap[base : base + 9] = mm(rows(0, 9), own).reshape(9, ROWS, 256)
        for by in range(3):
            f = 3 * by
            lap[base + f + 1 : base + f + 3] += mm(rows(f, 2), z_low).reshape(2, ROWS, 256)
            lap[base + f : base + f + 2] += mm(rows(f + 1, 2), z_high).reshape(2, ROWS, 256)
        lap[base + 3 : base + 9] += mm(rows(0, 6), y_low).reshape(6, ROWS, 256)
        lap[base : base + 6] += mm(rows(3, 6), y_high).reshape(6, ROWS, 256)

    pick = (
        lax.broadcasted_iota(jnp.int32, (ROWS, ATOMS), 0) // FUNCS
        == lax.broadcasted_iota(jnp.int32, (ROWS, ATOMS), 1)
    ).astype(F32).astype(BF16)
    first, last = sc[48], sc[49]

    def place(p, carry):
        offset = (p // 9) * 36 + (p // 3 % 3) * 6 + p % 3
        values = x_ref[p].astype(F32)
        p_lo = p - 9 * first
        p_hi = p + 9 * last
        keep_lo = jnp.where(p_lo >= 0, 1.0, 0.0).astype(F32)
        keep_hi = jnp.where(p_hi < 27, 1.0, 0.0).astype(F32)
        low = lo_ref[jnp.maximum(p_lo, 0)].astype(F32) * keep_lo
        high = hi_ref[jnp.minimum(p_hi, 26)].astype(F32) * keep_hi
        pot = mm(pick, v_ref[p])
        hphi = (-0.5 * (lap[p] + low + high) + pot * values).astype(BF16)
        for a in range(ATOMS):
            g = sc[a] + offset
            grid[g, ROWS + 4 * a : ROWS + 4 * a + 4, :] = x_ref[p, 4 * a : 4 * a + 4, :]
            grid[g, 4 * a : 4 * a + 4, :] = hphi[4 * a : 4 * a + 4, :]
        return carry

    lax.fori_loop(0, 27, place, 0)

    def place_band(q, carry):
        offset = (q // 9) * 36 + (q // 3 % 3) * 6 + q % 3
        for a in range(ATOMS):
            g = sc[16 + a] + offset + 36
            g = jnp.where(g < 0, GRID_BLOCKS, g)
            grid[g, 2 * ROWS + 4 * a : 2 * ROWS + 4 * a + 4, :] = bl_ref[q, 4 * a : 4 * a + 4, :]
            g = sc[32 + a] + offset
            g = jnp.where(g >= GRID_BLOCKS, GRID_BLOCKS, g)
            grid[g, 2 * ROWS + 4 * a : 2 * ROWS + 4 * a + 4, :] = bu_ref[q, 4 * a : 4 * a + 4, :]
        return carry

    lax.fori_loop(0, 18, place_band, 0)

    def grams(start, count, columns):
        batch = 6

        def step(i, acc):
            g = start + batch * i
            left = jnp.concatenate([grid[g + k, 0 : 2 * ROWS] for k in range(batch)], axis=1)
            right = jnp.concatenate([grid[g + k, ROWS : ROWS + columns] for k in range(batch)], axis=1)
            return acc + lax.dot_general(left, right, (((1,), (1,)), ((), ())), preferred_element_type=F32)

        return lax.fori_loop(0, count // batch, step, jnp.zeros((2 * ROWS, columns), F32))

    lower = grams(0, 72, 2 * ROWS)
    middle = grams(72, 36, ROWS)
    upper = grams(108, 72, 2 * ROWS)
    total = jnp.concatenate(
        [lower[:, ROWS:], lower[:, :ROWS] + middle + upper[:, :ROWS], upper[:, ROWS:]], axis=1
    )
    for a in range(ATOMS):
        out_ref[a, 0:4, :] = total[ROWS + 4 * a : ROWS + 4 * a + 4, :]
        out_ref[a, 4:8, :] = total[4 * a : 4 * a + 4, :]


def gram(scalars, x, lo, hi, bl, bu, v):
    vmem = pl.BlockSpec(memory_space=pltpu.VMEM)
    return pl.pallas_call(
        gram_kernel,
        out_shape=jax.ShapeDtypeStruct((ATOMS, 8, 3 * ROWS), F32),
        in_specs=[pl.BlockSpec(memory_space=pltpu.SMEM)] + [vmem] * 6,
        out_specs=vmem,
        scratch_shapes=[
            pltpu.VMEM((GRID_BLOCKS + 1, 3 * ROWS, 256), BF16),
            pltpu.VMEM((27, ROWS, 256), F32),
        ],
        compiler_params=pltpu.CompilerParams(vmem_limit_bytes=60 * 1024 * 1024),
    )(scalars, x, lo, hi, bl, bu, v)


def purify_kernel(
    n, part, k0, mask, metric, ham, pur,
    rs_buf, piece, ag, k0row, k0n, bblk, ball, y1, y1all, k1, k1all, mrow, mall,
    rs_s, rs_r, ag_s, ag_r, kr_s, kr_r, kn_s, kn_r, b_s, b_r, y_s, y_r, k_s, k_r, m_s, m_r,
):
    s = lax.axis_index("atoms")
    c = lax.axis_index("cols")
    up = lambda base, k: lax.rem(base + k + 2 * n, n)
    e = up(c - s, 1)
    active = e < 3

    def remote(src, dst, ss, rs, row, col):
        return pltpu.make_async_remote_copy(
            src_ref=src, dst_ref=dst, send_sem=ss, recv_sem=rs, device_id=(row, col), device_id_type=MESH
        )

    barrier = pltpu.get_barrier_semaphore()

    def hello(row, col):
        pl.semaphore_signal(barrier, inc=1, device_id=(row, col), device_id_type=MESH)

    for k in range(1, n):
        hello(s, up(c, k))
        hello(up(s, k), c)
    pairs = [(d, f) for d in range(-2, 3) for f in range(3)]

    @pl.when(active)
    def _():
        for d, f in pairs:
            t, v = up(s, d), up(s, d + f - 1)
            if d != 0:

                @pl.when(v != c)
                def _():
                    hello(t, v)

    pl.semaphore_wait(barrier, 2 * (n - 1) + jnp.where(active, 10, 0))

    rs_copies = []
    for k in range(1, n):
        col = up(c, k)
        copy = remote(part.at[col], rs_buf.at[k - 1], rs_s.at[k - 1], rs_r.at[k - 1], s, col)
        copy.start()
        rs_copies.append(copy)
    kn_copies = []
    for i, d in enumerate((1, -1)):
        copy = remote(k0, k0n.at[i], kn_s.at[i], kn_r.at[i], up(s, d), c)
        copy.start()
        kn_copies.append(copy)
    kr_copies = []
    for k in range(1, n):
        copy = remote(k0, k0row.at[c], kr_s.at[k - 1], kr_r.at[k - 1], s, up(c, k))
        copy.start()
        kr_copies.append(copy)
    k0row[c] = k0[...]

    total = part[c]
    for k in range(1, n):
        rs_copies[k - 1].wait_recv()
        total = total + rs_buf[k - 1]
    piece[...] = total
    ag[c] = total
    ag_copies = []
    for k in range(1, n):
        copy = remote(piece, ag.at[c], ag_s.at[k - 1], ag_r.at[k - 1], s, up(c, k))
        copy.start()
        ag_copies.append(copy)
    for copy in kn_copies:
        copy.wait_recv()
    panel = split(jnp.concatenate([k0n[0], k0[...], k0n[1]], axis=0))
    for copy in ag_copies:
        copy.wait_recv()
    for a in range(ATOMS):
        mrow[4 * a : 4 * a + 4, :] = ag[a, 0:4, :]
    m_own = mrow[...]
    bblk[...] = dot3(split(m_own), panel)
    b_copies = []
    for k in range(1, n):
        copy = remote(bblk, ball.at[s], b_s.at[k - 1], b_r.at[k - 1], up(s, k), c)
        copy.start()
        b_copies.append(copy)
    ball[s] = bblk[...]
    m_sends = []
    for i, d in enumerate((-2, -1, 1, 2)):
        target = up(s, d)
        wanted = up(c - target, 1) < 3
        copy = remote(mrow, mall.at[2 - d], m_s.at[i], m_r.at[i], target, c)
        m_sends.append((wanted, copy))

        @pl.when(wanted)
        def _():
            copy.start()

    inside = jnp.where(active, 1.0, 0.0).astype(F32)

    def block(matrix):
        left, mid, right = (matrix[:, ROWS * i : ROWS * (i + 1)] for i in range(3))
        return jnp.where(e == 0, left, jnp.where(e == 1, mid, right)) * inside

    metric[...] = block(m_own)
    for a in range(ATOMS):
        ham[4 * a : 4 * a + 4, :] = block(ag[a, 4:8, :])

    for copy in kr_copies:
        copy.wait_recv()
    k0cat = split(jnp.concatenate([k0row[t] for t in range(n)], axis=1))
    for copy in b_copies:
        copy.wait_recv()
    bcol = split(ball[...].reshape(n * ROWS, ROWS))
    y_own = dot3(k0cat, bcol)
    y1[...] = y_own
    y_sends = []
    for i in range(3):
        target = up(s, i - 1)
        wanted = target != c
        copy = remote(y1, y1all.at[c], y_s.at[i], y_r.at[c], s, target)
        y_sends.append((wanted, copy))

        @pl.when(wanted)
        def _():
            copy.start()

    pur[...] = jnp.zeros((ROWS, ROWS), F32)

    @pl.when(active)
    def _():
        y1all[c] = y_own
        for k in range(1, n):
            other = up(c, k)
            remote(y1, y1all.at[other], y_s.at[0], y_r.at[other], s, other).wait_recv()
        ycat = split(jnp.concatenate([y1all[t] for t in range(n)], axis=1))
        first = mask[...] * (3.0 * y_own - 2.0 * dot3(ycat, bcol))
        k1[...] = first
        for i, (d, f) in enumerate(pairs):
            t, v = up(s, d), up(s, d + f - 1)

            @pl.when(jnp.logical_not((d == 0) & (v == c)))
            def _():
                remote(k1, k1all.at[(2 - d) * 3 + e], k_s.at[i], k_r.at[(2 - d) * 3 + e], t, v).start()

        k1all[6 + e] = first
        mall[2] = m_own
        for i, d in enumerate((-2, -1, 1, 2)):
            remote(mrow, mall.at[2 - d], m_s.at[i], m_r.at[i], up(s, d), c).wait_recv()
        for i, (d, f) in enumerate(pairs):
            t, v = up(s, d), up(s, d + f - 1)

            @pl.when(jnp.logical_not((d == 0) & (v == c)))
            def _():
                remote(k1, k1all.at[i], k_s.at[i], k_r.at[i], t, v).wait_recv()

        kb = {}
        mb = {}
        for r in range(5):
            mr = mall[r]
            for f in range(3):
                kb[r, r + f] = k1all[3 * r + f]
                mb[r, r + f] = mr[:, ROWS * f : ROWS * f + ROWS]
        zero = jnp.zeros((ROWS, ROWS), F32)

        def window(blocks, rows, cols):
            return jnp.concatenate(
                [jnp.concatenate([blocks.get((r, q), zero) for q in cols], axis=1) for r in rows], axis=0
            )

        k_window = window(kb, range(5), range(7))
        m_window = split(window(mb, range(5), range(7)))
        x2 = dot3(split(window(kb, [2], [2, 3, 4])), split(window(mb, [1, 2, 3], range(1, 6))))
        y2 = dot3(split(x2), split(k_window))
        w2 = dot3(split(y2), m_window, (((1,), (1,)), ((), ())))
        columns = [
            jnp.concatenate([kb.get((r, q), zero) for r in range(5)], axis=0) for q in (2, 3, 4)
        ]
        kcol = jnp.where(e == 0, columns[0], jnp.where(e == 1, columns[1], columns[2]))
        y2s = jnp.where(
            e == 0, y2[:, 2 * ROWS : 3 * ROWS], jnp.where(e == 1, y2[:, 3 * ROWS : 4 * ROWS], y2[:, 4 * ROWS : 5 * ROWS])
        )
        pur[...] = mask[...] * (3.0 * y2s - 2.0 * dot3(split(w2), split(kcol)))
        for i, (d, f) in enumerate(pairs):
            t, v = up(s, d), up(s, d + f - 1)

            @pl.when(jnp.logical_not((d == 0) & (v == c)))
            def _():
                remote(k1, k1all.at[(2 - d) * 3 + e], k_s.at[i], k_r.at[i], t, v).wait_send()

    for copy in rs_copies + kn_copies + kr_copies + ag_copies + b_copies:
        copy.wait_send()
    for wanted, copy in m_sends + y_sends:

        @pl.when(wanted)
        def _():
            copy.wait_send()


def purify(n, part, kernel, mask):
    vmem = pl.BlockSpec(memory_space=pltpu.VMEM)
    block = jax.ShapeDtypeStruct((ROWS, ROWS), F32)
    dma = pltpu.SemaphoreType.DMA
    return pl.pallas_call(
        functools.partial(purify_kernel, n),
        out_shape=(block, block, block),
        in_specs=[vmem] * 3,
        out_specs=(vmem, vmem, vmem),
        scratch_shapes=[
            pltpu.VMEM((n - 1, 8, 3 * ROWS), F32),
            pltpu.VMEM((8, 3 * ROWS), F32),
            pltpu.VMEM((n, 8, 3 * ROWS), F32),
            pltpu.VMEM((n, ROWS, ROWS), F32),
            pltpu.VMEM((2, ROWS, ROWS), F32),
            pltpu.VMEM((ROWS, ROWS), F32),
            pltpu.VMEM((n, ROWS, ROWS), F32),
            pltpu.VMEM((ROWS, ROWS), F32),
            pltpu.VMEM((n, ROWS, ROWS), F32),
            pltpu.VMEM((ROWS, ROWS), F32),
            pltpu.VMEM((15, ROWS, ROWS), F32),
            pltpu.VMEM((ROWS, 3 * ROWS), F32),
            pltpu.VMEM((5, ROWS, 3 * ROWS), F32),
            dma((n,)), dma((n,)), dma((n,)), dma((n,)), dma((n,)), dma((n,)),
            dma((2,)), dma((2,)), dma((n,)), dma((n,)), dma((3,)), dma((n,)),
            dma((15,)), dma((15,)), dma((4,)), dma((4,)),
        ],
        compiler_params=pltpu.CompilerParams(
            collective_id=0, has_side_effects=True, vmem_limit_bytes=32 * 1024 * 1024
        ),
    )(part, kernel, mask)


def local(supports, potential, anchors, kernel):
    slab = lax.axis_index("atoms")
    col = lax.axis_index("cols")
    slabs = lax.axis_size("atoms")
    cols = lax.axis_size("cols")
    x = supports.transpose(2, 3, 0, 1, 4).reshape(27, ROWS, 256)
    v = potential.transpose(1, 2, 0, 3).reshape(27, ATOMS, 256)
    ring = [(i, (i + 1) % cols) for i in range(cols)]
    back = [(j, i) for i, j in ring]
    line = [(i, i + 1) for i in range(slabs - 1)]
    line_back = [(j, i) for i, j in line]
    lo = lax.ppermute(x, "cols", ring)
    hi = lax.ppermute(x, "cols", back)
    bl = lax.ppermute(x[9:], "atoms", line)
    bu = lax.ppermute(x[:18], "atoms", line_back)

    far = jnp.full((ATOMS, 3), -100, jnp.int32)
    padded = jnp.concatenate([far, anchors, -2 * far], axis=0)
    band = lax.dynamic_slice_in_dim(padded, slab * ATOMS, 3 * ATOMS, 0)
    corner = (band[:, 0] - 3 * slab) * 36 + band[:, 1] * 6 + band[:, 2]
    flags = jnp.stack([col == 0, col == cols - 1]).astype(jnp.int32)
    scalars = jnp.concatenate([corner[ATOMS : 2 * ATOMS], corner[:ATOMS], corner[2 * ATOMS :], flags])
    part = gram(scalars, x, lo, hi, bl, bu, v)

    rows = lax.dynamic_slice_in_dim(anchors, slab * ATOMS, ATOMS, 0)
    columns = lax.dynamic_slice_in_dim(anchors, col * ATOMS, ATOMS, 0)
    near = jnp.all(jnp.abs(columns[None] - rows[:, None]) <= 2, axis=-1).astype(F32)
    mask = jnp.broadcast_to(near[:, None, :, None], (ATOMS, FUNCS, ATOMS, FUNCS)).reshape(ROWS, ROWS)
    return purify(slabs, part, kernel, mask)


def solution(mesh):
    in_specs = (
        P("atoms", None, None, "cols", None),
        P("atoms", None, "cols", None),
        P(),
        P("atoms", "cols"),
    )
    out_specs = (P("atoms", "cols"), P("atoms", "cols"), P("atoms", "cols"))
    return jax.shard_map(local, mesh=mesh, in_specs=in_specs, out_specs=out_specs, check_vma=False)
```

```python
import functools

import jax
import jax.numpy as jnp
from jax import lax
from jax.experimental import pallas as pl
from jax.experimental.pallas import tpu as pltpu
from jax.sharding import PartitionSpec as P

MESH = pl.DeviceIdType.MESH
F32 = jnp.float32
BF16 = jnp.bfloat16
GRID_BLOCKS = 180
ATOMS = 16
FUNCS = 4
ROWS = ATOMS * FUNCS


def split(a):
    high = a.astype(BF16)
    return high, (a - high.astype(F32)).astype(BF16)


def dot3(left, right, dims=(((1,), (0,)), ((), ()))):
    lh, ll = left
    rh, rl = right
    mm = functools.partial(lax.dot_general, dimension_numbers=dims, preferred_element_type=F32)
    return mm(lh, rh) + (mm(lh, rl) + mm(ll, rh))


def shift_matrices():
    source = lax.broadcasted_iota(jnp.int32, (256, 256), 0)
    target = lax.broadcasted_iota(jnp.int32, (256, 256), 1)
    step = target - source
    z = target % 16
    one = jnp.float32(1.0)
    own = jnp.where(step == 0, -6.0, 0.0)
    own = own + jnp.where((step == 1) & (z != 0), one, 0.0)
    own = own + jnp.where((step == -1) & (z != 15), one, 0.0)
    own = own + jnp.where((step == 16) | (step == -16), one, 0.0)
    z_low = jnp.where((step == -15) & (z == 0), one, 0.0)
    z_high = jnp.where((step == 15) & (z == 15), one, 0.0)
    y_low = jnp.where(step == -240, one, 0.0)
    y_high = jnp.where(step == 240, one, 0.0)
    return [m.astype(BF16) for m in (own, z_low, z_high, y_low, y_high)]


def mm(a, b):
    return jnp.dot(a, b, preferred_element_type=F32)


def remote(src, dst, ss, rs, row, col):
    return pltpu.make_async_remote_copy(
        src_ref=src, dst_ref=dst, send_sem=ss, recv_sem=rs, device_id=(row, col), device_id_type=MESH
    )


def signal_barrier(row, col):
    pl.semaphore_signal(
        pltpu.get_barrier_semaphore(), inc=1, device_id=(row, col), device_id_type=MESH
    )


def exchange_kernel(n, x_ref, v_ref, phi, hphi, bl, bu, lo, hi, base, send, recv):
    s = lax.axis_index("atoms")
    c = lax.axis_index("cols")
    up = lambda at, k: lax.rem(at + k + n, n)
    for d in (1, -1):
        signal_barrier(s, up(c, d))
        signal_barrier(up(s, d), c)
    pl.semaphore_wait(pltpu.get_barrier_semaphore(), 4)
    copies = [
        remote(x_ref.at[9:27], bl.at[0:18], send.at[0], recv.at[0], up(s, 1), c),
        remote(x_ref.at[0:18], bu.at[0:18], send.at[1], recv.at[1], up(s, -1), c),
        remote(x_ref, lo, send.at[2], recv.at[2], s, up(c, 1)),
        remote(x_ref, hi, send.at[3], recv.at[3], s, up(c, -1)),
    ]
    for copy in copies:
        copy.start()
    empty = jnp.zeros((ROWS, 256), BF16)
    phi[27] = empty
    hphi[27] = empty
    bl[18] = empty
    bu[18] = empty
    phi[0:27] = x_ref[...]
    own, z_low, z_high, y_low, y_high = shift_matrices()
    for bx in range(3):
        first = 9 * bx
        rows = lambda at, count: x_ref[first + at : first + at + count].reshape(count * ROWS, 256)
        base[first : first + 9] = mm(rows(0, 9), own).reshape(9, ROWS, 256)
        for by in range(3):
            f = 3 * by
            base[first + f + 1 : first + f + 3] += mm(rows(f, 2), z_low).reshape(2, ROWS, 256)
            base[first + f : first + f + 2] += mm(rows(f + 1, 2), z_high).reshape(2, ROWS, 256)
        base[first + 3 : first + 9] += mm(rows(0, 6), y_low).reshape(6, ROWS, 256)
        base[first : first + 6] += mm(rows(3, 6), y_high).reshape(6, ROWS, 256)
    pick = (
        lax.broadcasted_iota(jnp.int32, (ROWS, ATOMS), 0) // FUNCS
        == lax.broadcasted_iota(jnp.int32, (ROWS, ATOMS), 1)
    ).astype(F32).astype(BF16)
    for p in range(27):
        base[p] = -0.5 * base[p] + mm(pick, v_ref[p]) * x_ref[p].astype(F32)
    copies[2].wait_recv()
    copies[3].wait_recv()
    first = jnp.where(c == 0, 1, 0)
    last = jnp.where(c == n - 1, 1, 0)
    for p in range(27):
        if p < 9:
            low = lo[p].astype(F32) * (1 - first).astype(F32)
        else:
            low = lo[p - 9 * first].astype(F32)
        if p >= 18:
            high = hi[p].astype(F32) * (1 - last).astype(F32)
        else:
            high = hi[p + 9 * last].astype(F32)
        hphi[p] = (base[p] - 0.5 * (low + high)).astype(BF16)
    copies[0].wait_recv()
    copies[1].wait_recv()
    for copy in copies:
        copy.wait_send()


def exchange(n, x, v):
    vmem = pl.BlockSpec(memory_space=pltpu.VMEM)
    blocks = lambda count: jax.ShapeDtypeStruct((count, ROWS, 256), BF16)
    return pl.pallas_call(
        functools.partial(exchange_kernel, n),
        out_shape=(blocks(28), blocks(28), blocks(19), blocks(19)),
        in_specs=[vmem] * 2,
        out_specs=(vmem,) * 4,
        scratch_shapes=[
            pltpu.VMEM((27, ROWS, 256), BF16),
            pltpu.VMEM((27, ROWS, 256), BF16),
            pltpu.VMEM((27, ROWS, 256), F32),
            pltpu.SemaphoreType.DMA((4,)),
            pltpu.SemaphoreType.DMA((4,)),
        ],
        compiler_params=pltpu.CompilerParams(
            collective_id=1, has_side_effects=True, vmem_limit_bytes=32 * 1024 * 1024
        ),
    )(x, v)


def pack(block):
    return jnp.concatenate([block[: ROWS // 2], block[ROWS // 2 :]], axis=1)


def unpack(packed):
    return jnp.concatenate([packed[:, :ROWS], packed[:, ROWS:]], axis=0)


def side_by_side(ref, n):
    lane = lax.broadcasted_iota(jnp.int32, (ROWS // 2, 2 * ROWS), 1) < ROWS
    tiles = []
    for t in range(0, n, 2):
        even, odd = ref[t], ref[t + 1]
        top = jnp.where(lane, even, pltpu.roll(odd, ROWS, 1))
        low = jnp.where(lane, pltpu.roll(even, ROWS, 1), odd)
        tiles.append(jnp.concatenate([top, low], axis=0))
    return jnp.concatenate(tiles, axis=1)


def stacked(ref, n):
    return jnp.concatenate([unpack(ref[t]) for t in range(n)], axis=0)


def gram_pass(table, phi, hphi, band, row, start, count, batch):
    def gather(ref, at, shift):
        tiles = []
        for i in range(4):
            picked = [
                ref[table[at + shift + 4 * i + j], 16 * i : 16 * i + 16, :] for j in range(4)
            ]
            tiles.append(
                jnp.where(
                    row < 8,
                    jnp.where(row < 4, picked[0], picked[1]),
                    jnp.where(row < 12, picked[2], picked[3]),
                )
            )
        return jnp.concatenate(tiles, axis=0)

    columns = ROWS if band is None else 2 * ROWS

    def step(i, acc):
        left, right = [], []
        for k in range(batch):
            at = (start + batch * i + k) * 32
            values = gather(phi, at, 0)
            left.append(jnp.concatenate([gather(hphi, at, 0), values], axis=0))
            if band is None:
                right.append(values)
            else:
                right.append(jnp.concatenate([values, gather(band, at, 16)], axis=0))
        left = jnp.concatenate(left, axis=1)
        right = jnp.concatenate(right, axis=1)
        return acc + lax.dot_general(left, right, (((1,), (1,)), ((), ())), preferred_element_type=F32)

    return lax.fori_loop(0, count // batch, step, jnp.zeros((2 * ROWS, columns), F32))


def purify_kernel(
    n, table, phi, hphi, bl, bu, k0, mask, out,
    part, k0p, rs_buf, piece, ag, k0row, k0n, bblk, ball, y1, y1all, k1, k1all, mrow, mall,
    rs_s, rs_r, ag_s, ag_r, kr_s, kr_r, kn_s, kn_r, b_s, b_r, y_s, y_r, k_s, k_r, m_s, m_r,
):
    s = lax.axis_index("atoms")
    c = lax.axis_index("cols")
    up = lambda base, k: lax.rem(base + k + 2 * n, n)
    e = up(c - s, 1)
    active = e < 3

    for k in range(1, n):
        signal_barrier(s, up(c, k))
        signal_barrier(up(s, k), c)
    pairs = [(d, f) for d in range(-2, 3) for f in range(3)]
    k0p[...] = pack(k0[...])
    row = lax.broadcasted_iota(jnp.int32, (16, 256), 0).astype(F32).astype(BF16)
    lower = gram_pass(table, phi, hphi, bl, row, 0, 72, 4)
    pl.semaphore_wait(pltpu.get_barrier_semaphore(), 2 * (n - 1))
    kn_copies = []
    for i, d in enumerate((1, -1)):
        copy = remote(k0p, k0n.at[i], kn_s.at[i], kn_r.at[i], up(s, d), c)
        copy.start()
        kn_copies.append(copy)
    kr_copies = []
    for k in range(1, n):
        copy = remote(k0p, k0row.at[c], kr_s.at[k - 1], kr_r.at[k - 1], s, up(c, k))
        copy.start()
        kr_copies.append(copy)
    k0row[c] = k0p[...]
    middle = gram_pass(table, phi, hphi, None, row, 72, 36, 4)
    upper = gram_pass(table, phi, hphi, bu, row, 108, 72, 4)
    sums = jnp.concatenate(
        [lower[:, ROWS:], lower[:, :ROWS] + middle + upper[:, :ROWS], upper[:, ROWS:]], axis=1
    )
    for a in range(ATOMS):
        part[a, 0:4, :] = sums[ROWS + 4 * a : ROWS + 4 * a + 4, :]
        part[a, 4:8, :] = sums[4 * a : 4 * a + 4, :]

    rs_copies = []
    for k in range(1, n):
        col = up(c, k)
        copy = remote(part.at[col], rs_buf.at[k - 1], rs_s.at[k - 1], rs_r.at[k - 1], s, col)
        copy.start()
        rs_copies.append(copy)
    total = part[c]
    for k in range(1, n):
        rs_copies[k - 1].wait_recv()
        total = total + rs_buf[k - 1]
    piece[...] = total
    ag[c] = total
    ag_copies = []
    for k in range(1, n):
        copy = remote(piece, ag.at[c], ag_s.at[k - 1], ag_r.at[k - 1], s, up(c, k))
        copy.start()
        ag_copies.append(copy)
    for copy in kn_copies:
        copy.wait_recv()
    panel = split(jnp.concatenate([unpack(k0n[0]), k0[...], unpack(k0n[1])], axis=0))
    for copy in ag_copies:
        copy.wait_recv()
    for a in range(ATOMS):
        mrow[4 * a : 4 * a + 4, :] = ag[a, 0:4, :]
    m_own = mrow[...]
    bblk[...] = pack(dot3(split(m_own), panel))
    b_copies = []
    for k in range(1, n):
        copy = remote(bblk, ball.at[s], b_s.at[k - 1], b_r.at[k - 1], up(s, k), c)
        copy.start()
        b_copies.append(copy)
    ball[s] = bblk[...]
    m_sends = []
    for i, d in enumerate((-2, -1, 1, 2)):
        target = up(s, d)
        wanted = up(c - target, 1) < 3
        copy = remote(mrow, mall.at[2 - d], m_s.at[i], m_r.at[i], target, c)
        m_sends.append((wanted, copy))

        @pl.when(wanted)
        def _():
            copy.start()

    inside = jnp.where(active, 1.0, 0.0).astype(F32)

    def block(matrix):
        left, mid, right = (matrix[:, ROWS * i : ROWS * (i + 1)] for i in range(3))
        return jnp.where(e == 0, left, jnp.where(e == 1, mid, right)) * inside

    out[0] = block(m_own)
    for a in range(ATOMS):
        out[1, 4 * a : 4 * a + 4, :] = block(ag[a, 4:8, :])

    for copy in kr_copies:
        copy.wait_recv()
    k0cat = split(side_by_side(k0row, n))
    for copy in b_copies:
        copy.wait_recv()
    bcol = split(stacked(ball, n))
    y_own = dot3(k0cat, bcol)
    y1[...] = pack(y_own)
    y_sends = []
    for i in range(3):
        target = up(s, i - 1)
        wanted = target != c
        copy = remote(y1, y1all.at[c], y_s.at[i], y_r.at[c], s, target)
        y_sends.append((wanted, copy))

        @pl.when(wanted)
        def _():
            copy.start()

    out[2] = jnp.zeros((ROWS, ROWS), F32)

    @pl.when(active)
    def _():
        y1all[c] = y1[...]
        for k in range(1, n):
            other = up(c, k)
            remote(y1, y1all.at[other], y_s.at[0], y_r.at[other], s, other).wait_recv()
        ycat = split(side_by_side(y1all, n))
        first = mask[...] * (3.0 * y_own - 2.0 * dot3(ycat, bcol))
        k1[...] = pack(first)
        for i, (d, f) in enumerate(pairs):
            t, v = up(s, d), up(s, d + f - 1)

            @pl.when(jnp.logical_not((d == 0) & (v == c)))
            def _():
                remote(k1, k1all.at[(2 - d) * 3 + e], k_s.at[i], k_r.at[(2 - d) * 3 + e], t, v).start()

        k1all[6 + e] = k1[...]
        mall[2] = m_own
        for i, d in enumerate((-2, -1, 1, 2)):
            remote(mrow, mall.at[2 - d], m_s.at[i], m_r.at[i], up(s, d), c).wait_recv()
        for i, (d, f) in enumerate(pairs):
            t, v = up(s, d), up(s, d + f - 1)

            @pl.when(jnp.logical_not((d == 0) & (v == c)))
            def _():
                remote(k1, k1all.at[i], k_s.at[i], k_r.at[i], t, v).wait_recv()

        kb = {}
        mb = {}
        for r in range(5):
            mr = mall[r]
            for f in range(3):
                kb[r, r + f] = unpack(k1all[3 * r + f])
                mb[r, r + f] = mr[:, ROWS * f : ROWS * f + ROWS]
        zero = jnp.zeros((ROWS, ROWS), F32)

        def window(blocks, rows, cols):
            return jnp.concatenate(
                [jnp.concatenate([blocks.get((r, q), zero) for q in cols], axis=1) for r in rows], axis=0
            )

        k_window = window(kb, range(5), range(7))
        m_window = split(window(mb, range(5), range(7)))
        x2 = dot3(split(window(kb, [2], [2, 3, 4])), split(window(mb, [1, 2, 3], range(1, 6))))
        y2 = dot3(split(x2), split(k_window))
        w2 = dot3(split(y2), m_window, (((1,), (1,)), ((), ())))
        columns = [
            jnp.concatenate([kb.get((r, q), zero) for r in range(5)], axis=0) for q in (2, 3, 4)
        ]
        kcol = jnp.where(e == 0, columns[0], jnp.where(e == 1, columns[1], columns[2]))
        y2s = jnp.where(
            e == 0, y2[:, 2 * ROWS : 3 * ROWS], jnp.where(e == 1, y2[:, 3 * ROWS : 4 * ROWS], y2[:, 4 * ROWS : 5 * ROWS])
        )
        out[2] = mask[...] * (3.0 * y2s - 2.0 * dot3(split(w2), split(kcol)))
        for i, (d, f) in enumerate(pairs):
            t, v = up(s, d), up(s, d + f - 1)

            @pl.when(jnp.logical_not((d == 0) & (v == c)))
            def _():
                remote(k1, k1all.at[(2 - d) * 3 + e], k_s.at[i], k_r.at[i], t, v).wait_send()

    for copy in rs_copies + kn_copies + kr_copies + ag_copies + b_copies:
        copy.wait_send()
    for wanted, copy in m_sends + y_sends:

        @pl.when(wanted)
        def _():
            copy.wait_send()


def purify(n, table, phi, hphi, bl, bu, kernel, mask):
    vmem = pl.BlockSpec(memory_space=pltpu.VMEM)
    dma = pltpu.SemaphoreType.DMA
    half = lambda *lead: pltpu.VMEM((*lead, ROWS // 2, 2 * ROWS), F32)
    return pl.pallas_call(
        functools.partial(purify_kernel, n),
        out_shape=jax.ShapeDtypeStruct((3, ROWS, ROWS), F32),
        in_specs=[pl.BlockSpec(memory_space=pltpu.SMEM)] + [vmem] * 6,
        out_specs=vmem,
        scratch_shapes=[
            pltpu.VMEM((n, 8, 3 * ROWS), F32),
            half(),
            pltpu.VMEM((n - 1, 8, 3 * ROWS), F32),
            pltpu.VMEM((8, 3 * ROWS), F32),
            pltpu.VMEM((n, 8, 3 * ROWS), F32),
            half(n),
            half(2),
            half(),
            half(n),
            half(),
            half(n),
            half(),
            half(15),
            pltpu.VMEM((ROWS, 3 * ROWS), F32),
            pltpu.VMEM((5, ROWS, 3 * ROWS), F32),
            dma((n,)), dma((n,)), dma((n,)), dma((n,)), dma((n,)), dma((n,)),
            dma((2,)), dma((2,)), dma((n,)), dma((n,)), dma((3,)), dma((n,)),
            dma((15,)), dma((15,)), dma((4,)), dma((4,)),
        ],
        compiler_params=pltpu.CompilerParams(
            collective_id=0, has_side_effects=True, vmem_limit_bytes=40 * 1024 * 1024
        ),
    )(table, phi, hphi, bl, bu, kernel, mask)


def block_table(band, slab):
    blocks = jnp.arange(GRID_BLOCKS, dtype=jnp.int32)
    place = jnp.stack([blocks // 36 + 3 * slab, blocks // 6 % 6, blocks % 6], axis=-1)
    offset = place[:, None, :] - band[None, :, :]
    inside = jnp.all((offset >= 0) & (offset <= 2), axis=-1)
    index = offset[..., 0] * 9 + offset[..., 1] * 3 + offset[..., 2]
    own = jnp.where(inside, index, 27)[:, ATOMS : 2 * ATOMS]
    lower = jnp.where(inside, index - 9, 18)[:, :ATOMS]
    upper = jnp.where(inside, index, 18)[:, 2 * ATOMS :]
    other = jnp.where(blocks[:, None] < 72, lower, upper)
    return jnp.concatenate([own, other], axis=1).reshape(-1)


def local(supports, potential, anchors, kernel):
    slab = lax.axis_index("atoms")
    col = lax.axis_index("cols")
    slabs = lax.axis_size("atoms")
    x = supports.transpose(2, 3, 0, 1, 4).reshape(27, ROWS, 256)
    v = potential.transpose(1, 2, 0, 3).reshape(27, ATOMS, 256)
    phi, hphi, bl, bu = exchange(slabs, x, v)
    far = jnp.full((ATOMS, 3), -100, jnp.int32)
    padded = jnp.concatenate([far, anchors, -2 * far], axis=0)
    band = lax.dynamic_slice_in_dim(padded, slab * ATOMS, 3 * ATOMS, 0)
    table = block_table(band, slab)
    rows = lax.dynamic_slice_in_dim(anchors, slab * ATOMS, ATOMS, 0)
    columns = lax.dynamic_slice_in_dim(anchors, col * ATOMS, ATOMS, 0)
    near = jnp.all(jnp.abs(columns[None] - rows[:, None]) <= 2, axis=-1).astype(F32)
    mask = jnp.broadcast_to(near[:, None, :, None], (ATOMS, FUNCS, ATOMS, FUNCS)).reshape(ROWS, ROWS)
    out = purify(slabs, table, phi, hphi, bl, bu, kernel, mask)
    return out[0], out[1], out[2]


def solution(mesh):
    in_specs = (
        P("atoms", None, None, "cols", None),
        P("atoms", None, "cols", None),
        P(),
        P("atoms", "cols"),
    )
    out_specs = (P("atoms", "cols"), P("atoms", "cols"), P("atoms", "cols"))
    return jax.shard_map(local, mesh=mesh, in_specs=in_specs, out_specs=out_specs, check_vma=False)
```

```python
import functools

import jax
import jax.numpy as jnp
from jax import lax
from jax.experimental import pallas as pl
from jax.experimental.pallas import tpu as pltpu
from jax.sharding import PartitionSpec as P

MESH = pl.DeviceIdType.MESH
F32 = jnp.float32
BF16 = jnp.bfloat16
GRID_BLOCKS = 180
BATCH = 12
ATOMS = 16
FUNCS = 4
ROWS = ATOMS * FUNCS


def split(a):
    high = a.astype(BF16)
    return high, (a - high.astype(F32)).astype(BF16)


def dot3(left, right, dims=(((1,), (0,)), ((), ()))):
    lh, ll = left
    rh, rl = right
    mm = functools.partial(lax.dot_general, dimension_numbers=dims, preferred_element_type=F32)
    return mm(lh, rh) + (mm(lh, rl) + mm(ll, rh))


def shift_matrices():
    source = lax.broadcasted_iota(jnp.int32, (256, 256), 0)
    target = lax.broadcasted_iota(jnp.int32, (256, 256), 1)
    step = target - source
    z = target % 16
    one = jnp.float32(1.0)
    own = jnp.where(step == 0, -6.0, 0.0)
    own = own + jnp.where((step == 1) & (z != 0), one, 0.0)
    own = own + jnp.where((step == -1) & (z != 15), one, 0.0)
    own = own + jnp.where((step == 16) | (step == -16), one, 0.0)
    z_low = jnp.where((step == -15) & (z == 0), one, 0.0)
    z_high = jnp.where((step == 15) & (z == 15), one, 0.0)
    y_low = jnp.where(step == -240, one, 0.0)
    y_high = jnp.where(step == 240, one, 0.0)
    return [m.astype(BF16) for m in (own, z_low, z_high, y_low, y_high)]


def mm(a, b):
    return jnp.dot(a, b, preferred_element_type=F32)


def remote(src, dst, ss, rs, row, col):
    return pltpu.make_async_remote_copy(
        src_ref=src, dst_ref=dst, send_sem=ss, recv_sem=rs, device_id=(row, col), device_id_type=MESH
    )


def signal_barrier(row, col):
    pl.semaphore_signal(
        pltpu.get_barrier_semaphore(), inc=1, device_id=(row, col), device_id_type=MESH
    )


def interleave(phi, hphi):
    head = lax.broadcasted_iota(jnp.int32, phi.shape, 0) % 8 < 4
    even = jnp.where(head, phi, pltpu.roll(hphi, 4, 0))
    odd = jnp.where(head, pltpu.roll(phi, ROWS - 4, 0), hphi)
    return jnp.concatenate([even, odd], axis=0).astype(BF16)


def exchange_kernel(n, x_ref, v_hbm, both, bl, bu, v_ref, lo, hi, base, v_sem, send, recv):
    s = lax.axis_index("atoms")
    c = lax.axis_index("cols")
    up = lambda at, k: lax.rem(at + k + n, n)
    load = pltpu.make_async_copy(v_hbm, v_ref, v_sem)
    load.start()
    for d in (1, -1):
        signal_barrier(s, up(c, d))
        signal_barrier(up(s, d), c)
    pl.semaphore_wait(pltpu.get_barrier_semaphore(), 4)
    copies = [
        remote(x_ref.at[9:27], bl.at[0:18], send.at[0], recv.at[0], up(s, 1), c),
        remote(x_ref.at[0:18], bu.at[0:18], send.at[1], recv.at[1], up(s, -1), c),
        remote(x_ref, lo, send.at[2], recv.at[2], s, up(c, 1)),
        remote(x_ref, hi, send.at[3], recv.at[3], s, up(c, -1)),
    ]
    for copy in copies:
        copy.start()
    empty = jnp.zeros((ROWS, 256), BF16)
    both[27] = jnp.concatenate([empty, empty], axis=0)
    bl[18] = empty
    bu[18] = empty
    own, z_low, z_high, y_low, y_high = shift_matrices()
    for bx in range(3):
        first = 9 * bx
        rows = lambda at, count: x_ref[first + at : first + at + count].reshape(count * ROWS, 256)
        base[first : first + 9] = mm(rows(0, 9), own).reshape(9, ROWS, 256)
        for by in range(3):
            f = 3 * by
            base[first + f + 1 : first + f + 3] += mm(rows(f, 2), z_low).reshape(2, ROWS, 256)
            base[first + f : first + f + 2] += mm(rows(f + 1, 2), z_high).reshape(2, ROWS, 256)
        base[first + 3 : first + 9] += mm(rows(0, 6), y_low).reshape(6, ROWS, 256)
        base[first : first + 6] += mm(rows(3, 6), y_high).reshape(6, ROWS, 256)
    pick = (
        lax.broadcasted_iota(jnp.int32, (ROWS, ATOMS), 0) // FUNCS
        == lax.broadcasted_iota(jnp.int32, (ROWS, ATOMS), 1)
    ).astype(F32).astype(BF16)
    load.wait()
    for p in range(27):
        base[p] = -0.5 * base[p] + mm(pick, v_ref[p]) * x_ref[p].astype(F32)
    copies[2].wait_recv()
    copies[3].wait_recv()
    first = jnp.where(c == 0, 1, 0)
    last = jnp.where(c == n - 1, 1, 0)
    for p in range(27):
        if p < 9:
            low = lo[p].astype(F32) * (1 - first).astype(F32)
        else:
            low = lo[p - 9 * first].astype(F32)
        if p >= 18:
            high = hi[p].astype(F32) * (1 - last).astype(F32)
        else:
            high = hi[p + 9 * last].astype(F32)
        both[p] = interleave(x_ref[p].astype(F32), base[p] - 0.5 * (low + high))
    copies[0].wait_recv()
    copies[1].wait_recv()
    for copy in copies:
        copy.wait_send()


def exchange(n, x, v):
    vmem = pl.BlockSpec(memory_space=pltpu.VMEM)
    blocks = lambda count, rows=ROWS: jax.ShapeDtypeStruct((count, rows, 256), BF16)
    return pl.pallas_call(
        functools.partial(exchange_kernel, n),
        out_shape=(blocks(28, 2 * ROWS), blocks(19), blocks(19)),
        in_specs=[vmem, pl.BlockSpec(memory_space=pl.ANY)],
        out_specs=(vmem,) * 3,
        scratch_shapes=[
            pltpu.VMEM((27, ATOMS, 256), BF16),
            pltpu.VMEM((27, ROWS, 256), BF16),
            pltpu.VMEM((27, ROWS, 256), BF16),
            pltpu.VMEM((27, ROWS, 256), F32),
            pltpu.SemaphoreType.DMA,
            pltpu.SemaphoreType.DMA((4,)),
            pltpu.SemaphoreType.DMA((4,)),
        ],
        compiler_params=pltpu.CompilerParams(
            collective_id=1, has_side_effects=True, vmem_limit_bytes=16 * 1024 * 1024
        ),
    )(x, v)


def pack(block):
    return jnp.concatenate([block[: ROWS // 2], block[ROWS // 2 :]], axis=1)


def unpack(packed):
    return jnp.concatenate([packed[:, :ROWS], packed[:, ROWS:]], axis=0)


def side_by_side(ref, n):
    lane = lax.broadcasted_iota(jnp.int32, (ROWS // 2, 2 * ROWS), 1) < ROWS
    tiles = []
    for t in range(0, n, 2):
        even, odd = ref[t], ref[t + 1]
        top = jnp.where(lane, even, pltpu.roll(odd, ROWS, 1))
        low = jnp.where(lane, pltpu.roll(even, ROWS, 1), odd)
        tiles.append(jnp.concatenate([top, low], axis=0))
    return jnp.concatenate(tiles, axis=1)


def stacked(ref, n):
    return jnp.concatenate([unpack(ref[t]) for t in range(n)], axis=0)


def gram_pass(table, both, band, row, start, count):
    def own(at, k):
        tiles = []
        for i in range(8):
            first, second = (4 * i, 4 * i + 2) if i < 4 else (4 * i - 15, 4 * i - 13)
            rows = slice(16 * i, 16 * i + 16)
            tiles.append(
                jnp.where(
                    row < 8,
                    both[table[at, 32 * k + first], rows, :],
                    both[table[at, 32 * k + second], rows, :],
                )
            )
        return tiles

    def near(at, k):
        tiles = []
        for i in range(4):
            rows = slice(16 * i, 16 * i + 16)
            picked = [band[table[at, 32 * k + 16 + 4 * i + j], rows, :] for j in range(4)]
            tiles.append(
                jnp.where(
                    row < 8,
                    jnp.where(row < 4, picked[0], picked[1]),
                    jnp.where(row < 12, picked[2], picked[3]),
                )
            )
        return tiles

    columns = 2 * ROWS if band is None else 3 * ROWS

    def step(i, acc):
        left, right = [], []
        for k in range(BATCH):
            tiles = own(start // BATCH + i, k)
            left.append(jnp.concatenate(tiles, axis=0))
            if band is not None:
                tiles = tiles + near(start // BATCH + i, k)
            right.append(jnp.concatenate(tiles, axis=0))
        left = jnp.concatenate(left, axis=1)
        right = jnp.concatenate(right, axis=1)
        return acc + lax.dot_general(left, right, (((1,), (1,)), ((), ())), preferred_element_type=F32)

    return lax.fori_loop(0, count // BATCH, step, jnp.zeros((2 * ROWS, columns), F32))


def purify_kernel(
    n, table, both, bl, bu, k0, near, out,
    part, k0p, rs_buf, piece, ag, k0row, k0n, bblk, ball, y1, y1all, k1, k1all, mrow, mall,
    rs_s, rs_r, ag_s, ag_r, kr_s, kr_r, kn_s, kn_r, b_s, b_r, y_s, y_r, k_s, k_r, m_s, m_r,
):
    s = lax.axis_index("atoms")
    c = lax.axis_index("cols")
    up = lambda base, k: lax.rem(base + k + 2 * n, n)
    e = up(c - s, 1)
    active = e < 3

    for k in range(1, n):
        signal_barrier(s, up(c, k))
        signal_barrier(up(s, k), c)
    pairs = [(d, f) for d in range(-2, 3) for f in range(3)]
    k0p[...] = pack(k0[...])
    spread = (
        lax.broadcasted_iota(jnp.int32, (ROWS, ATOMS), 0) // FUNCS
        == lax.broadcasted_iota(jnp.int32, (ROWS, ATOMS), 1)
    ).astype(F32).astype(BF16)
    mask = lax.dot_general(
        mm(spread, near[...].astype(BF16)).astype(BF16),
        spread,
        (((1,), (1,)), ((), ())),
        preferred_element_type=F32,
    )
    row = lax.broadcasted_iota(jnp.int32, (16, 256), 0).astype(F32).astype(BF16)
    lower = gram_pass(table, both, bl, row, 0, 72)
    pl.semaphore_wait(pltpu.get_barrier_semaphore(), 2 * (n - 1))
    kn_copies = []
    for i, d in enumerate((1, -1)):
        copy = remote(k0p, k0n.at[i], kn_s.at[i], kn_r.at[i], up(s, d), c)
        copy.start()
        kn_copies.append(copy)
    kr_copies = []
    for k in range(1, n):
        copy = remote(k0p, k0row.at[c], kr_s.at[k - 1], kr_r.at[k - 1], s, up(c, k))
        copy.start()
        kr_copies.append(copy)
    k0row[c] = k0p[...]
    middle = gram_pass(table, both, None, row, 72, 36)
    upper = gram_pass(table, both, bu, row, 108, 72)
    mine = lower[:, : 2 * ROWS] + middle + upper[:, : 2 * ROWS]
    source = lax.broadcasted_iota(jnp.int32, (2 * ROWS, ROWS), 0)
    target = lax.broadcasted_iota(jnp.int32, (2 * ROWS, ROWS), 1)
    atom = target // 4
    place = 8 * (atom // 2 + 8 * (atom % 2)) + target % 4
    mine = jnp.dot(
        mine, (source == place).astype(F32), precision=lax.Precision.HIGHEST, preferred_element_type=F32
    )
    sums = jnp.concatenate([lower[:, 2 * ROWS :], mine, upper[:, 2 * ROWS :]], axis=1)
    for a in range(ATOMS):
        at = 8 * (a // 2 + 8 * (a % 2))
        part[a] = sums[at : at + 8, :]

    rs_copies = []
    for k in range(1, n):
        col = up(c, k)
        copy = remote(part.at[col], rs_buf.at[k - 1], rs_s.at[k - 1], rs_r.at[k - 1], s, col)
        copy.start()
        rs_copies.append(copy)
    total = part[c]
    for k in range(1, n):
        rs_copies[k - 1].wait_recv()
        total = total + rs_buf[k - 1]
    piece[...] = total
    ag[c] = total
    ag_copies = []
    for k in range(1, n):
        copy = remote(piece, ag.at[c], ag_s.at[k - 1], ag_r.at[k - 1], s, up(c, k))
        copy.start()
        ag_copies.append(copy)
    for copy in kn_copies:
        copy.wait_recv()
    panel = split(jnp.concatenate([unpack(k0n[0]), k0[...], unpack(k0n[1])], axis=0))
    for copy in ag_copies:
        copy.wait_recv()
    for a in range(ATOMS):
        mrow[4 * a : 4 * a + 4, :] = ag[a, 0:4, :]
    m_own = mrow[...]
    bblk[...] = pack(dot3(split(m_own), panel))
    b_copies = []
    for k in range(1, n):
        copy = remote(bblk, ball.at[s], b_s.at[k - 1], b_r.at[k - 1], up(s, k), c)
        copy.start()
        b_copies.append(copy)
    ball[s] = bblk[...]
    inside = jnp.where(active, 1.0, 0.0).astype(F32)

    def block(matrix):
        left, mid, right = (matrix[:, ROWS * i : ROWS * (i + 1)] for i in range(3))
        return jnp.where(e == 0, left, jnp.where(e == 1, mid, right)) * inside

    out[0] = block(m_own)
    for a in range(ATOMS):
        out[1, 4 * a : 4 * a + 4, :] = block(ag[a, 4:8, :])

    for copy in kr_copies:
        copy.wait_recv()
    k0cat = split(side_by_side(k0row, n))
    for copy in b_copies:
        copy.wait_recv()
    bcol = split(stacked(ball, n))
    y_own = dot3(k0cat, bcol)
    y1[...] = pack(y_own)
    y_sends = []
    for i in range(3):
        target = up(s, i - 1)
        wanted = target != c
        copy = remote(y1, y1all.at[c], y_s.at[i], y_r.at[c], s, target)
        y_sends.append((wanted, copy))

        @pl.when(wanted)
        def _():
            copy.start()

    m_sends = []
    for i, d in enumerate((-2, -1, 1, 2)):
        target = up(s, d)
        wanted = up(c - target, 1) < 3
        copy = remote(mrow, mall.at[2 - d], m_s.at[i], m_r.at[i], target, c)
        m_sends.append((wanted, copy))

        @pl.when(wanted)
        def _():
            copy.start()

    out[2] = jnp.zeros((ROWS, ROWS), F32)

    @pl.when(active)
    def _():
        y1all[c] = y1[...]
        for k in range(1, n):
            other = up(c, k)
            remote(y1, y1all.at[other], y_s.at[0], y_r.at[other], s, other).wait_recv()
        ycat = split(side_by_side(y1all, n))
        first = mask * (3.0 * y_own - 2.0 * dot3(ycat, bcol))
        k1[...] = pack(first)
        for i, (d, f) in enumerate(pairs):
            t, v = up(s, d), up(s, d + f - 1)

            @pl.when(jnp.logical_not((d == 0) & (v == c)))
            def _():
                remote(k1, k1all.at[(2 - d) * 3 + e], k_s.at[i], k_r.at[(2 - d) * 3 + e], t, v).start()

        k1all[6 + e] = k1[...]
        mall[2] = m_own
        for i, d in enumerate((-2, -1, 1, 2)):
            remote(mrow, mall.at[2 - d], m_s.at[i], m_r.at[i], up(s, d), c).wait_recv()
        for i, (d, f) in enumerate(pairs):
            t, v = up(s, d), up(s, d + f - 1)

            @pl.when(jnp.logical_not((d == 0) & (v == c)))
            def _():
                remote(k1, k1all.at[i], k_s.at[i], k_r.at[i], t, v).wait_recv()

        kb = {}
        mb = {}
        for r in range(5):
            mr = mall[r]
            for f in range(3):
                kb[r, r + f] = unpack(k1all[3 * r + f])
                mb[r, r + f] = mr[:, ROWS * f : ROWS * f + ROWS]
        zero = jnp.zeros((ROWS, ROWS), F32)

        def window(blocks, rows, cols):
            return jnp.concatenate(
                [jnp.concatenate([blocks.get((r, q), zero) for q in cols], axis=1) for r in rows], axis=0
            )

        k_window = window(kb, range(5), range(7))
        m_window = split(window(mb, range(5), range(7)))
        x2 = dot3(split(window(kb, [2], [2, 3, 4])), split(window(mb, [1, 2, 3], range(1, 6))))
        y2 = dot3(split(x2), split(k_window))
        w2 = dot3(split(y2), m_window, (((1,), (1,)), ((), ())))
        columns = [
            jnp.concatenate([kb.get((r, q), zero) for r in range(5)], axis=0) for q in (2, 3, 4)
        ]
        kcol = jnp.where(e == 0, columns[0], jnp.where(e == 1, columns[1], columns[2]))
        y2s = jnp.where(
            e == 0, y2[:, 2 * ROWS : 3 * ROWS], jnp.where(e == 1, y2[:, 3 * ROWS : 4 * ROWS], y2[:, 4 * ROWS : 5 * ROWS])
        )
        out[2] = mask * (3.0 * y2s - 2.0 * dot3(split(w2), split(kcol)))
        for i, (d, f) in enumerate(pairs):
            t, v = up(s, d), up(s, d + f - 1)

            @pl.when(jnp.logical_not((d == 0) & (v == c)))
            def _():
                remote(k1, k1all.at[(2 - d) * 3 + e], k_s.at[i], k_r.at[i], t, v).wait_send()

    for copy in rs_copies + kn_copies + kr_copies + ag_copies + b_copies:
        copy.wait_send()
    for wanted, copy in m_sends + y_sends:

        @pl.when(wanted)
        def _():
            copy.wait_send()


def purify(n, table, both, bl, bu, kernel, near):
    vmem = pl.BlockSpec(memory_space=pltpu.VMEM)
    dma = pltpu.SemaphoreType.DMA
    half = lambda *lead: pltpu.VMEM((*lead, ROWS // 2, 2 * ROWS), F32)
    return pl.pallas_call(
        functools.partial(purify_kernel, n),
        out_shape=jax.ShapeDtypeStruct((3, ROWS, ROWS), F32),
        in_specs=[pl.BlockSpec(memory_space=pltpu.SMEM)] + [vmem] * 5,
        out_specs=vmem,
        scratch_shapes=[
            pltpu.VMEM((n, 8, 3 * ROWS), F32),
            half(),
            pltpu.VMEM((n - 1, 8, 3 * ROWS), F32),
            pltpu.VMEM((8, 3 * ROWS), F32),
            pltpu.VMEM((n, 8, 3 * ROWS), F32),
            half(n),
            half(2),
            half(),
            half(n),
            half(),
            half(n),
            half(),
            half(15),
            pltpu.VMEM((ROWS, 3 * ROWS), F32),
            pltpu.VMEM((5, ROWS, 3 * ROWS), F32),
            dma((n,)), dma((n,)), dma((n,)), dma((n,)), dma((n,)), dma((n,)),
            dma((2,)), dma((2,)), dma((n,)), dma((n,)), dma((3,)), dma((n,)),
            dma((15,)), dma((15,)), dma((4,)), dma((4,)),
        ],
        compiler_params=pltpu.CompilerParams(
            collective_id=0, has_side_effects=True, vmem_limit_bytes=16 * 1024 * 1024
        ),
    )(table, both, bl, bu, kernel, near)


def block_table(band, slab):
    blocks = jnp.arange(GRID_BLOCKS, dtype=jnp.int32)
    place = jnp.stack([blocks // 36 + 3 * slab, blocks // 6 % 6, blocks % 6], axis=-1)
    offset = place[:, None, :] - band[None, :, :]
    inside = jnp.all((offset >= 0) & (offset <= 2), axis=-1)
    index = offset[..., 0] * 9 + offset[..., 1] * 3 + offset[..., 2]
    own = jnp.where(inside, index, 27)[:, ATOMS : 2 * ATOMS]
    lower = jnp.where(inside, index - 9, 18)[:, :ATOMS]
    upper = jnp.where(inside, index, 18)[:, 2 * ATOMS :]
    other = jnp.where(blocks[:, None] < 72, lower, upper)
    return jnp.concatenate([own, other], axis=1).reshape(GRID_BLOCKS // BATCH, 32 * BATCH)


def local(supports, potential, anchors, kernel):
    slab = lax.axis_index("atoms")
    col = lax.axis_index("cols")
    slabs = lax.axis_size("atoms")
    x = supports.transpose(2, 3, 0, 1, 4).reshape(27, ROWS, 256)
    v = potential.transpose(1, 2, 0, 3).reshape(27, ATOMS, 256)
    both, bl, bu = exchange(slabs, x, v)
    far = jnp.full((ATOMS, 3), -100, jnp.int32)
    padded = jnp.concatenate([far, anchors, -2 * far], axis=0)
    band = lax.dynamic_slice_in_dim(padded, slab * ATOMS, 3 * ATOMS, 0)
    table = block_table(band, slab)
    rows = lax.dynamic_slice_in_dim(anchors, slab * ATOMS, ATOMS, 0)
    columns = lax.dynamic_slice_in_dim(anchors, col * ATOMS, ATOMS, 0)
    near = jnp.all(jnp.abs(columns[None] - rows[:, None]) <= 2, axis=-1).astype(F32)
    out = purify(slabs, table, both, bl, bu, kernel, near)
    return out[0], out[1], out[2]


def solution(mesh):
    in_specs = (
        P("atoms", None, None, "cols", None),
        P("atoms", None, "cols", None),
        P(),
        P("atoms", "cols"),
    )
    out_specs = (P("atoms", "cols"), P("atoms", "cols"), P("atoms", "cols"))
    return jax.shard_map(local, mesh=mesh, in_specs=in_specs, out_specs=out_specs, check_vma=False)
```

```python
import functools

import jax
import jax.numpy as jnp
from jax import lax
from jax.experimental import pallas as pl
from jax.experimental.pallas import tpu as pltpu
from jax.sharding import PartitionSpec as P

MESH = pl.DeviceIdType.MESH
F32 = jnp.float32
BF16 = jnp.bfloat16
ATOMS = 16
FUNCS = 4
ROWS = ATOMS * FUNCS


def split(a):
    high = a.astype(BF16)
    return high, (a - high.astype(F32)).astype(BF16)


def dot3(left, right, dims=(((1,), (0,)), ((), ()))):
    lh, ll = left
    rh, rl = right
    mm = functools.partial(lax.dot_general, dimension_numbers=dims, preferred_element_type=F32)
    return mm(lh, rh) + (mm(lh, rl) + mm(ll, rh))


def shift_matrices():
    source = lax.broadcasted_iota(jnp.int32, (256, 256), 0)
    target = lax.broadcasted_iota(jnp.int32, (256, 256), 1)
    step = target - source
    z = target % 16
    one = jnp.float32(1.0)
    own = jnp.where(step == 0, -6.0, 0.0)
    own = own + jnp.where((step == 1) & (z != 0), one, 0.0)
    own = own + jnp.where((step == -1) & (z != 15), one, 0.0)
    own = own + jnp.where((step == 16) | (step == -16), one, 0.0)
    z_low = jnp.where((step == -15) & (z == 0), one, 0.0)
    z_high = jnp.where((step == 15) & (z == 15), one, 0.0)
    y_low = jnp.where(step == -240, one, 0.0)
    y_high = jnp.where(step == 240, one, 0.0)
    return [m.astype(BF16) for m in (own, z_low, z_high, y_low, y_high)]


def mm(a, b):
    return jnp.dot(a, b, preferred_element_type=F32)


def remote(src, dst, ss, rs, row, col):
    return pltpu.make_async_remote_copy(
        src_ref=src, dst_ref=dst, send_sem=ss, recv_sem=rs, device_id=(row, col), device_id_type=MESH
    )


def signal_barrier(row, col):
    pl.semaphore_signal(
        pltpu.get_barrier_semaphore(), inc=1, device_id=(row, col), device_id_type=MESH
    )


def interleave(phi, hphi):
    head = lax.broadcasted_iota(jnp.int32, phi.shape, 0) % 8 < 4
    even = jnp.where(head, phi, pltpu.roll(hphi, 4, 0))
    odd = jnp.where(head, pltpu.roll(phi, ROWS - 4, 0), hphi)
    return jnp.concatenate([even, odd], axis=0).astype(BF16)


def pack(block):
    return jnp.concatenate([block[: ROWS // 2], block[ROWS // 2 :]], axis=1)


def unpack(packed):
    return jnp.concatenate([packed[:, :ROWS], packed[:, ROWS:]], axis=0)


def side_by_side(ref, n):
    lane = lax.broadcasted_iota(jnp.int32, (ROWS // 2, 2 * ROWS), 1) < ROWS
    tiles = []
    for t in range(0, n, 2):
        even, odd = ref[t], ref[t + 1]
        top = jnp.where(lane, even, pltpu.roll(odd, ROWS, 1))
        low = jnp.where(lane, pltpu.roll(even, ROWS, 1), odd)
        tiles.append(jnp.concatenate([top, low], axis=0))
    return jnp.concatenate(tiles, axis=1)


def stacked(ref, n):
    return jnp.concatenate([unpack(ref[t]) for t in range(n)], axis=0)


def gram_pass(table, both, band, row, start, count):
    def own(at, k):
        runs = [both.at[pl.ds(table[at, 32 * k + a], 6)] for a in range(ATOMS)]

        def tiles(z):
            out = []
            for i in range(8):
                first, second = (4 * i, 4 * i + 2) if i < 4 else (4 * i - 15, 4 * i - 13)
                rows = slice(16 * i, 16 * i + 16)
                out.append(jnp.where(row < 8, runs[first][z, rows, :], runs[second][z, rows, :]))
            return out

        return tiles

    def near(at, k):
        runs = [band.at[pl.ds(table[at, 32 * k + 16 + a], 6)] for a in range(ATOMS)]

        def tiles(z):
            out = []
            for i in range(4):
                rows = slice(16 * i, 16 * i + 16)
                picked = [runs[4 * i + j][z, rows, :] for j in range(4)]
                out.append(
                    jnp.where(
                        row < 8,
                        jnp.where(row < 4, picked[0], picked[1]),
                        jnp.where(row < 12, picked[2], picked[3]),
                    )
                )
            return out

        return tiles

    columns = 2 * ROWS if band is None else 3 * ROWS

    def step(i, acc):
        left, right = [], []
        for k in range(2):
            mine = own(start + i, k)
            others = None if band is None else near(start + i, k)
            for z in range(6):
                tiles = mine(z)
                left.append(jnp.concatenate(tiles, axis=0))
                if others is not None:
                    tiles = tiles + others(z)
                right.append(jnp.concatenate(tiles, axis=0))
        left = jnp.concatenate(left, axis=1)
        right = jnp.concatenate(right, axis=1)
        return acc + lax.dot_general(left, right, (((1,), (1,)), ((), ())), preferred_element_type=F32)

    return lax.fori_loop(0, count, step, jnp.zeros((2 * ROWS, columns), F32))


def slab_kernel(
    n, table, x_ref, v_hbm, k0, near, out,
    both, bl, bu, lo, hi, base, v_ref,
    part, k0p, rs_buf, piece, ag, k0row, k0n, bblk, ball, y1, y1all, k1, k1all, mrow, mall,
    v_sem, band_s, band_r, halo_s, halo_r, known,
    rs_s, rs_r, ag_s, ag_r, kr_s, kr_r, kn_s, kn_r, b_s, b_r, y_s, y_r, k_s, k_r, m_s, m_r,
):
    s = lax.axis_index("atoms")
    c = lax.axis_index("cols")
    up = lambda at, k: lax.rem(at + k + 2 * n, n)
    e = up(c - s, 1)
    active = e < 3
    pairs = [(d, f) for d in range(-2, 3) for f in range(3)]
    load = pltpu.make_async_copy(v_hbm, v_ref, v_sem)
    load.start()
    for d in (1, -1):
        signal_barrier(s, up(c, d))
        signal_barrier(up(s, d), c)
    k0p[...] = pack(k0[...])
    pl.semaphore_wait(pltpu.get_barrier_semaphore(), 4)

    halo = [
        remote(x_ref, lo, halo_s.at[0], halo_r.at[0], s, up(c, 1)),
        remote(x_ref, hi, halo_s.at[1], halo_r.at[1], s, up(c, -1)),
    ]
    for copy in halo:
        copy.start()
    band_copies = []
    for k in range(6):
        source, target = x_ref.at[9 + 3 * k : 12 + 3 * k], bl.at[9 * k + 3 : 9 * k + 6]
        band_copies.append(remote(source, target, band_s.at[k], band_r.at[k], up(s, 1), c))
        source, target = x_ref.at[3 * k : 3 * k + 3], bu.at[9 * k + 3 : 9 * k + 6]
        band_copies.append(remote(source, target, band_s.at[6 + k], band_r.at[6 + k], up(s, -1), c))
    for copy in band_copies:
        copy.start()
    kn_copies = []
    for i, d in enumerate((1, -1)):
        copy = remote(k0p, k0n.at[i], kn_s.at[i], kn_r.at[i], up(s, d), c)
        copy.start()
        kn_copies.append(copy)

    def tell(step):
        for d in (1 << step, -(1 << step)):
            pl.semaphore_signal(known.at[step], inc=1, device_id=(s, up(c, d)), device_id_type=MESH)
            pl.semaphore_signal(known.at[3 + step], inc=1, device_id=(up(s, d), c), device_id_type=MESH)

    def learn(step):
        pl.semaphore_wait(known.at[step], 2)
        pl.semaphore_wait(known.at[3 + step], 2)

    tell(0)
    own, z_low, z_high, y_low, y_high = shift_matrices()
    for bx in range(3):
        first = 9 * bx
        rows = lambda at, count: x_ref[first + at : first + at + count].reshape(count * ROWS, 256)
        base[first : first + 9] = mm(rows(0, 9), own).reshape(9, ROWS, 256)
        for by in range(3):
            f = 3 * by
            base[first + f + 1 : first + f + 3] += mm(rows(f, 2), z_low).reshape(2, ROWS, 256)
            base[first + f : first + f + 2] += mm(rows(f + 1, 2), z_high).reshape(2, ROWS, 256)
        base[first + 3 : first + 9] += mm(rows(0, 6), y_low).reshape(6, ROWS, 256)
        base[first : first + 6] += mm(rows(3, 6), y_high).reshape(6, ROWS, 256)
    learn(0)
    tell(1)
    spread = (
        lax.broadcasted_iota(jnp.int32, (ROWS, ATOMS), 0) // FUNCS
        == lax.broadcasted_iota(jnp.int32, (ROWS, ATOMS), 1)
    ).astype(F32).astype(BF16)
    load.wait()
    for p in range(27):
        base[p] = -0.5 * base[p] + mm(spread, v_ref[p]) * x_ref[p].astype(F32)
    learn(1)
    tell(2)
    for at in range(0, 81, 9):
        both[at : at + 3] = jnp.zeros((3, 2 * ROWS, 256), BF16)
        both[at + 6 : at + 9] = jnp.zeros((3, 2 * ROWS, 256), BF16)
    both[81:90] = jnp.zeros((9, 2 * ROWS, 256), BF16)
    for ref in (bl, bu):
        for at in range(0, 54, 9):
            ref[at : at + 3] = jnp.zeros((3, ROWS, 256), BF16)
            ref[at + 6 : at + 9] = jnp.zeros((3, ROWS, 256), BF16)
        ref[54:63] = jnp.zeros((9, ROWS, 256), BF16)
    mask = lax.dot_general(
        mm(spread, near[...].astype(BF16)).astype(BF16),
        spread,
        (((1,), (1,)), ((), ())),
        preferred_element_type=F32,
    )
    learn(2)
    kr_copies = []
    for k in range(1, n):
        copy = remote(k0p, k0row.at[c], kr_s.at[k - 1], kr_r.at[k - 1], s, up(c, k))
        copy.start()
        kr_copies.append(copy)
    k0row[c] = k0p[...]
    for copy in halo:
        copy.wait_recv()
    first = jnp.where(c == 0, 1, 0)
    last = jnp.where(c == n - 1, 1, 0)
    for p in range(27):
        if p < 9:
            low = lo[p].astype(F32) * (1 - first).astype(F32)
        else:
            low = lo[p - 9 * first].astype(F32)
        if p >= 18:
            high = hi[p].astype(F32) * (1 - last).astype(F32)
        else:
            high = hi[p + 9 * last].astype(F32)
        both[9 * (p // 3) + 3 + p % 3] = interleave(x_ref[p].astype(F32), base[p] - 0.5 * (low + high))
    row = lax.broadcasted_iota(jnp.int32, (16, 256), 0).astype(F32).astype(BF16)
    middle = gram_pass(table, both, None, row, 6, 3)
    for copy in band_copies:
        copy.wait_recv()
    lower = gram_pass(table, both, bl, row, 0, 6)
    upper = gram_pass(table, both, bu, row, 9, 6)
    mine = lower[:, : 2 * ROWS] + middle + upper[:, : 2 * ROWS]
    source = lax.broadcasted_iota(jnp.int32, (2 * ROWS, ROWS), 0)
    target = lax.broadcasted_iota(jnp.int32, (2 * ROWS, ROWS), 1)
    atom = target // 4
    place = 8 * (atom // 2 + 8 * (atom % 2)) + target % 4
    mine = jnp.dot(
        mine, (source == place).astype(F32), precision=lax.Precision.HIGHEST, preferred_element_type=F32
    )
    sums = jnp.concatenate([lower[:, 2 * ROWS :], mine, upper[:, 2 * ROWS :]], axis=1)
    for a in range(ATOMS):
        at = 8 * (a // 2 + 8 * (a % 2))
        part[a] = sums[at : at + 8, :]

    rs_copies = []
    for k in range(1, n):
        col = up(c, k)
        copy = remote(part.at[col], rs_buf.at[k - 1], rs_s.at[k - 1], rs_r.at[k - 1], s, col)
        copy.start()
        rs_copies.append(copy)
    total = part[c]
    for k in range(1, n):
        rs_copies[k - 1].wait_recv()
        total = total + rs_buf[k - 1]
    piece[...] = total
    ag[c] = total
    ag_copies = []
    for k in range(1, n):
        copy = remote(piece, ag.at[c], ag_s.at[k - 1], ag_r.at[k - 1], s, up(c, k))
        copy.start()
        ag_copies.append(copy)
    for copy in kn_copies:
        copy.wait_recv()
    panel = split(jnp.concatenate([unpack(k0n[0]), k0[...], unpack(k0n[1])], axis=0))
    for copy in ag_copies:
        copy.wait_recv()
    for a in range(ATOMS):
        mrow[4 * a : 4 * a + 4, :] = ag[a, 0:4, :]
    m_own = mrow[...]
    bblk[...] = pack(dot3(split(m_own), panel))
    b_copies = []
    for k in range(1, n):
        copy = remote(bblk, ball.at[s], b_s.at[k - 1], b_r.at[k - 1], up(s, k), c)
        copy.start()
        b_copies.append(copy)
    ball[s] = bblk[...]
    inside = jnp.where(active, 1.0, 0.0).astype(F32)

    def block(matrix):
        left, mid, right = (matrix[:, ROWS * i : ROWS * (i + 1)] for i in range(3))
        return jnp.where(e == 0, left, jnp.where(e == 1, mid, right)) * inside

    out[0] = block(m_own)
    for a in range(ATOMS):
        out[1, 4 * a : 4 * a + 4, :] = block(ag[a, 4:8, :])

    for copy in kr_copies:
        copy.wait_recv()
    k0cat = split(side_by_side(k0row, n))
    for copy in b_copies:
        copy.wait_recv()
    bcol = split(stacked(ball, n))
    y_own = dot3(k0cat, bcol)
    y1[...] = pack(y_own)
    y_sends = []
    for i in range(3):
        target = up(s, i - 1)
        wanted = target != c
        copy = remote(y1, y1all.at[c], y_s.at[i], y_r.at[c], s, target)
        y_sends.append((wanted, copy))

        @pl.when(wanted)
        def _():
            copy.start()

    m_sends = []
    for i, d in enumerate((-2, -1, 1, 2)):
        target = up(s, d)
        wanted = up(c - target, 1) < 3
        copy = remote(mrow, mall.at[2 - d], m_s.at[i], m_r.at[i], target, c)
        m_sends.append((wanted, copy))

        @pl.when(wanted)
        def _():
            copy.start()

    out[2] = jnp.zeros((ROWS, ROWS), F32)

    @pl.when(active)
    def _():
        y1all[c] = y1[...]
        for k in range(1, n):
            other = up(c, k)
            remote(y1, y1all.at[other], y_s.at[0], y_r.at[other], s, other).wait_recv()
        ycat = split(side_by_side(y1all, n))
        first = mask * (3.0 * y_own - 2.0 * dot3(ycat, bcol))
        k1[...] = pack(first)
        for i, (d, f) in enumerate(pairs):
            t, v = up(s, d), up(s, d + f - 1)

            @pl.when(jnp.logical_not((d == 0) & (v == c)))
            def _():
                remote(k1, k1all.at[(2 - d) * 3 + e], k_s.at[i], k_r.at[(2 - d) * 3 + e], t, v).start()

        k1all[6 + e] = k1[...]
        mall[2] = m_own
        for i, d in enumerate((-2, -1, 1, 2)):
            remote(mrow, mall.at[2 - d], m_s.at[i], m_r.at[i], up(s, d), c).wait_recv()
        for i, (d, f) in enumerate(pairs):
            t, v = up(s, d), up(s, d + f - 1)

            @pl.when(jnp.logical_not((d == 0) & (v == c)))
            def _():
                remote(k1, k1all.at[i], k_s.at[i], k_r.at[i], t, v).wait_recv()

        kb = {}
        mb = {}
        for r in range(5):
            mr = mall[r]
            for f in range(3):
                kb[r, r + f] = unpack(k1all[3 * r + f])
                mb[r, r + f] = mr[:, ROWS * f : ROWS * f + ROWS]
        zero = jnp.zeros((ROWS, ROWS), F32)

        def window(blocks, rows, cols):
            return jnp.concatenate(
                [jnp.concatenate([blocks.get((r, q), zero) for q in cols], axis=1) for r in rows], axis=0
            )

        k_window = window(kb, range(5), range(7))
        m_window = split(window(mb, range(5), range(7)))
        x2 = dot3(split(window(kb, [2], [2, 3, 4])), split(window(mb, [1, 2, 3], range(1, 6))))
        y2 = dot3(split(x2), split(k_window))
        w2 = dot3(split(y2), m_window, (((1,), (1,)), ((), ())))
        columns = [
            jnp.concatenate([kb.get((r, q), zero) for r in range(5)], axis=0) for q in (2, 3, 4)
        ]
        kcol = jnp.where(e == 0, columns[0], jnp.where(e == 1, columns[1], columns[2]))
        y2s = jnp.where(
            e == 0, y2[:, 2 * ROWS : 3 * ROWS], jnp.where(e == 1, y2[:, 3 * ROWS : 4 * ROWS], y2[:, 4 * ROWS : 5 * ROWS])
        )
        out[2] = mask * (3.0 * y2s - 2.0 * dot3(split(w2), split(kcol)))
        for i, (d, f) in enumerate(pairs):
            t, v = up(s, d), up(s, d + f - 1)

            @pl.when(jnp.logical_not((d == 0) & (v == c)))
            def _():
                remote(k1, k1all.at[(2 - d) * 3 + e], k_s.at[i], k_r.at[i], t, v).wait_send()

    for copy in halo + band_copies + rs_copies + kn_copies + kr_copies + ag_copies + b_copies:
        copy.wait_send()
    for wanted, copy in m_sends + y_sends:

        @pl.when(wanted)
        def _():
            copy.wait_send()


def slab_program(n, table, x, v, kernel, near):
    vmem = pl.BlockSpec(memory_space=pltpu.VMEM)
    dma = pltpu.SemaphoreType.DMA
    blocks = lambda count, rows=ROWS, kind=BF16: pltpu.VMEM((count, rows, 256), kind)
    half = lambda *lead: pltpu.VMEM((*lead, ROWS // 2, 2 * ROWS), F32)
    return pl.pallas_call(
        functools.partial(slab_kernel, n),
        out_shape=jax.ShapeDtypeStruct((3, ROWS, ROWS), F32),
        in_specs=[
            pl.BlockSpec(memory_space=pltpu.SMEM),
            vmem,
            pl.BlockSpec(memory_space=pl.ANY),
            vmem,
            vmem,
        ],
        out_specs=vmem,
        scratch_shapes=[
            blocks(90, 2 * ROWS),
            blocks(63),
            blocks(63),
            blocks(27),
            blocks(27),
            blocks(27, kind=F32),
            blocks(27, ATOMS),
            pltpu.VMEM((n, 8, 3 * ROWS), F32),
            half(),
            pltpu.VMEM((n - 1, 8, 3 * ROWS), F32),
            pltpu.VMEM((8, 3 * ROWS), F32),
            pltpu.VMEM((n, 8, 3 * ROWS), F32),
            half(n),
            half(2),
            half(),
            half(n),
            half(),
            half(n),
            half(),
            half(15),
            pltpu.VMEM((ROWS, 3 * ROWS), F32),
            pltpu.VMEM((5, ROWS, 3 * ROWS), F32),
            dma, dma((12,)), dma((12,)), dma((2,)), dma((2,)),
            pltpu.SemaphoreType.REGULAR((6,)),
            dma((n,)), dma((n,)), dma((n,)), dma((n,)), dma((n,)), dma((n,)),
            dma((2,)), dma((2,)), dma((n,)), dma((n,)), dma((3,)), dma((n,)),
            dma((15,)), dma((15,)), dma((4,)), dma((4,)),
        ],
        compiler_params=pltpu.CompilerParams(
            collective_id=0, has_side_effects=True, vmem_limit_bytes=40 * 1024 * 1024
        ),
    )(table, x, v, kernel, near)


def run_table(band, slab):
    cells = jnp.arange(30, dtype=jnp.int32)
    place = jnp.stack([cells // 6 + 3 * slab, cells % 6], axis=-1)
    offset = place[:, None, :] - band[None, :, :2]
    inside = jnp.all((offset >= 0) & (offset <= 2), axis=-1)
    start = (offset[..., 0] * 3 + offset[..., 1]) * 9 + 3 - band[None, :, 2]
    own = jnp.where(inside, start, 81)[:, ATOMS : 2 * ATOMS]
    lower = jnp.where(inside, start - 27, 54)[:, :ATOMS]
    upper = jnp.where(inside, start, 54)[:, 2 * ATOMS :]
    other = jnp.where(cells[:, None] < 12, lower, jnp.where(cells[:, None] < 18, 54, upper))
    return jnp.concatenate([own, other], axis=1).reshape(15, 64)


def local(supports, potential, anchors, kernel):
    slab = lax.axis_index("atoms")
    col = lax.axis_index("cols")
    x = supports.transpose(2, 3, 0, 1, 4).reshape(27, ROWS, 256)
    v = potential.transpose(1, 2, 0, 3).reshape(27, ATOMS, 256)
    far = jnp.full((ATOMS, 3), -100, jnp.int32)
    padded = jnp.concatenate([far, anchors, -2 * far], axis=0)
    band = lax.dynamic_slice_in_dim(padded, slab * ATOMS, 3 * ATOMS, 0)
    table = run_table(band, slab)
    rows = lax.dynamic_slice_in_dim(anchors, slab * ATOMS, ATOMS, 0)
    columns = lax.dynamic_slice_in_dim(anchors, col * ATOMS, ATOMS, 0)
    near = jnp.all(jnp.abs(columns[None] - rows[:, None]) <= 2, axis=-1).astype(F32)
    out = slab_program(lax.axis_size("atoms"), table, x, v, kernel, near)
    return out[0], out[1], out[2]


def solution(mesh):
    in_specs = (
        P("atoms", None, None, "cols", None),
        P("atoms", None, "cols", None),
        P(),
        P("atoms", "cols"),
    )
    out_specs = (P("atoms", "cols"), P("atoms", "cols"), P("atoms", "cols"))
    return jax.shard_map(local, mesh=mesh, in_specs=in_specs, out_specs=out_specs, check_vma=False)
```

```python
import functools

import jax
import jax.numpy as jnp
from jax import lax
from jax.experimental import pallas as pl
from jax.experimental.pallas import tpu as pltpu
from jax.sharding import PartitionSpec as P

MESH = pl.DeviceIdType.MESH
F32 = jnp.float32
BF16 = jnp.bfloat16
ATOMS = 16
FUNCS = 4
ROWS = ATOMS * FUNCS


def split(a):
    high = a.astype(BF16)
    return high, (a - high.astype(F32)).astype(BF16)


def dot3(left, right, dims=(((1,), (0,)), ((), ()))):
    lh, ll = left
    rh, rl = right
    mm = functools.partial(lax.dot_general, dimension_numbers=dims, preferred_element_type=F32)
    return mm(lh, rh) + (mm(lh, rl) + mm(ll, rh))


def shift_matrices():
    source = lax.broadcasted_iota(jnp.int32, (256, 256), 0)
    target = lax.broadcasted_iota(jnp.int32, (256, 256), 1)
    step = target - source
    z = target % 16
    one = jnp.float32(1.0)
    own = jnp.where(step == 0, -6.0, 0.0)
    own = own + jnp.where((step == 1) & (z != 0), one, 0.0)
    own = own + jnp.where((step == -1) & (z != 15), one, 0.0)
    own = own + jnp.where((step == 16) | (step == -16), one, 0.0)
    z_low = jnp.where((step == -15) & (z == 0), one, 0.0)
    z_high = jnp.where((step == 15) & (z == 15), one, 0.0)
    y_low = jnp.where(step == -240, one, 0.0)
    y_high = jnp.where(step == 240, one, 0.0)
    return [m.astype(BF16) for m in (own, z_low, z_high, y_low, y_high)]


def mm(a, b):
    return jnp.dot(a, b, preferred_element_type=F32)


def remote(src, dst, ss, rs, row, col):
    return pltpu.make_async_remote_copy(
        src_ref=src, dst_ref=dst, send_sem=ss, recv_sem=rs, device_id=(row, col), device_id_type=MESH
    )


def signal_barrier(row, col):
    pl.semaphore_signal(
        pltpu.get_barrier_semaphore(), inc=1, device_id=(row, col), device_id_type=MESH
    )


def pack(block):
    return jnp.concatenate([block[: ROWS // 2], block[ROWS // 2 :]], axis=1)


def unpack(packed):
    return jnp.concatenate([packed[:, :ROWS], packed[:, ROWS:]], axis=0)


def side_by_side(ref, n):
    lane = lax.broadcasted_iota(jnp.int32, (ROWS // 2, 2 * ROWS), 1) < ROWS
    tiles = []
    for t in range(0, n, 2):
        even, odd = ref[t], ref[t + 1]
        top = jnp.where(lane, even, pltpu.roll(odd, ROWS, 1))
        low = jnp.where(lane, pltpu.roll(even, ROWS, 1), odd)
        tiles.append(jnp.concatenate([top, low], axis=0))
    return jnp.concatenate(tiles, axis=1)


def stacked(ref, n):
    return jnp.concatenate([unpack(ref[t]) for t in range(n)], axis=0)


def gather(table, row, ref, at, shift):
    runs = [ref.at[pl.ds(table[at, shift + a], 6)] for a in range(ATOMS)]

    def block(z):
        tiles = []
        for i in range(4):
            rows = slice(16 * i, 16 * i + 16)
            picked = [runs[4 * i + j][z, rows, :] for j in range(4)]
            tiles.append(
                jnp.where(
                    row < 8,
                    jnp.where(row < 4, picked[0], picked[1]),
                    jnp.where(row < 12, picked[2], picked[3]),
                )
            )
        return jnp.concatenate(tiles, axis=0)

    return block


def products(table, start, count, left, own, band):
    row = lax.broadcasted_iota(jnp.int32, (16, 256), 0).astype(F32).astype(BF16)
    columns = ROWS * ((own is not None) + (band is not None))

    def step(i, acc):
        lefts, rights = [], []
        for k in range(2):
            at = start + i
            left_of = gather(table, row, left, at, 32 * k)
            own_of = None if own is None or own is left else gather(table, row, own, at, 32 * k)
            band_of = None if band is None else gather(table, row, band, at, 32 * k + 16)
            for z in range(6):
                first = left_of(z)
                lefts.append(first)
                parts = []
                if own is not None:
                    parts.append(first if own is left else own_of(z))
                if band is not None:
                    parts.append(band_of(z))
                rights.append(jnp.concatenate(parts, axis=0))
        return acc + lax.dot_general(
            jnp.concatenate(lefts, axis=1),
            jnp.concatenate(rights, axis=1),
            (((1,), (1,)), ((), ())),
            preferred_element_type=F32,
        )

    return lax.fori_loop(0, count, step, jnp.zeros((ROWS, columns), F32))


def to_pieces(ref, matrix):
    for a in range(ATOMS):
        ref[a, 0:4, :] = matrix[4 * a : 4 * a + 4, : 2 * ROWS]
        ref[a, 4:8, 0:ROWS] = matrix[4 * a : 4 * a + 4, 2 * ROWS :]
        ref[a, 4:8, ROWS:] = jnp.zeros((4, ROWS), F32)


def from_pieces(ref, rows):
    for a in range(ATOMS):
        rows[4 * a : 4 * a + 4, 0 : 2 * ROWS] = ref[a, 0:4, :]
        rows[4 * a : 4 * a + 4, 2 * ROWS :] = ref[a, 4:8, 0:ROWS]


def slab_kernel(
    n, table, x_ref, v_hbm, k0, near, out,
    phi, hphi, bl, bu, lo, hi, base, v_ref,
    part, k0p, rs_buf, piece, ag, part_h, rs_buf_h, piece_h, ag_h, hrow, k0row, k0n, bblk, ball, y1, y1all, k1, k1all, mrow, mall,
    v_sem, band_s, band_r, halo_s, halo_r, known,
    rs_s, rs_r, ag_s, ag_r, rh_s, rh_r, ah_s, ah_r, kr_s, kr_r, kn_s, kn_r, b_s, b_r, y_s, y_r, k_s, k_r, m_s, m_r,
):
    s = lax.axis_index("atoms")
    c = lax.axis_index("cols")
    up = lambda at, k: lax.rem(at + k + 2 * n, n)
    e = up(c - s, 1)
    active = e < 3
    pairs = [(d, f) for d in range(-2, 3) for f in range(3)]
    load = pltpu.make_async_copy(v_hbm, v_ref, v_sem)
    load.start()
    for d in (1, -1):
        signal_barrier(s, up(c, d))
        signal_barrier(up(s, d), c)
    k0p[...] = pack(k0[...])
    pl.semaphore_wait(pltpu.get_barrier_semaphore(), 4)

    def tell(step):
        for d in (1 << step, -(1 << step)):
            pl.semaphore_signal(known.at[step], inc=1, device_id=(s, up(c, d)), device_id_type=MESH)
            pl.semaphore_signal(known.at[3 + step], inc=1, device_id=(up(s, d), c), device_id_type=MESH)

    def learn(step):
        pl.semaphore_wait(known.at[step], 2)
        pl.semaphore_wait(known.at[3 + step], 2)

    tell(0)
    halo = [
        remote(x_ref, lo, halo_s.at[0], halo_r.at[0], s, up(c, 1)),
        remote(x_ref, hi, halo_s.at[1], halo_r.at[1], s, up(c, -1)),
    ]
    for copy in halo:
        copy.start()
    band_copies = []
    for k in range(6):
        source, target = x_ref.at[9 + 3 * k : 12 + 3 * k], bl.at[9 * k + 3 : 9 * k + 6]
        band_copies.append(remote(source, target, band_s.at[k], band_r.at[k], up(s, 1), c))
        source, target = x_ref.at[3 * k : 3 * k + 3], bu.at[9 * k + 3 : 9 * k + 6]
        band_copies.append(remote(source, target, band_s.at[6 + k], band_r.at[6 + k], up(s, -1), c))
    for copy in band_copies:
        copy.start()
    kn_copies = []
    for i, d in enumerate((1, -1)):
        copy = remote(k0p, k0n.at[i], kn_s.at[i], kn_r.at[i], up(s, d), c)
        copy.start()
        kn_copies.append(copy)

    learn(0)
    tell(1)
    own, z_low, z_high, y_low, y_high = shift_matrices()
    for bx in range(3):
        first = 9 * bx
        rows = lambda at, count: x_ref[first + at : first + at + count].reshape(count * ROWS, 256)
        base[first : first + 9] = mm(rows(0, 9), own).reshape(9, ROWS, 256)
        for by in range(3):
            f = 3 * by
            base[first + f + 1 : first + f + 3] += mm(rows(f, 2), z_low).reshape(2, ROWS, 256)
            base[first + f : first + f + 2] += mm(rows(f + 1, 2), z_high).reshape(2, ROWS, 256)
        base[first + 3 : first + 9] += mm(rows(0, 6), y_low).reshape(6, ROWS, 256)
        base[first : first + 6] += mm(rows(3, 6), y_high).reshape(6, ROWS, 256)
        if bx == 0:
            learn(1)
            tell(2)
    spread = (
        lax.broadcasted_iota(jnp.int32, (ROWS, ATOMS), 0) // FUNCS
        == lax.broadcasted_iota(jnp.int32, (ROWS, ATOMS), 1)
    ).astype(F32).astype(BF16)
    learn(2)
    kr_copies = []
    for k in range(1, n):
        copy = remote(k0p, k0row.at[c], kr_s.at[k - 1], kr_r.at[k - 1], s, up(c, k))
        copy.start()
        kr_copies.append(copy)
    k0row[c] = k0p[...]
    load.wait()
    for p in range(27):
        base[p] = -0.5 * base[p] + mm(spread, v_ref[p]) * x_ref[p].astype(F32)
    for p in range(27):
        phi[9 * (p // 3) + 3 + p % 3] = x_ref[p]
    for ref in (phi, hphi):
        for at in range(0, 81, 9):
            ref[at : at + 3] = jnp.zeros((3, ROWS, 256), BF16)
            ref[at + 6 : at + 9] = jnp.zeros((3, ROWS, 256), BF16)
        ref[81:90] = jnp.zeros((9, ROWS, 256), BF16)
    for ref in (bl, bu):
        for at in range(0, 54, 9):
            ref[at : at + 3] = jnp.zeros((3, ROWS, 256), BF16)
            ref[at + 6 : at + 9] = jnp.zeros((3, ROWS, 256), BF16)
        ref[54:63] = jnp.zeros((9, ROWS, 256), BF16)
    mask = lax.dot_general(
        mm(spread, near[...].astype(BF16)).astype(BF16),
        spread,
        (((1,), (1,)), ((), ())),
        preferred_element_type=F32,
    )
    s_own = products(table, 0, 15, phi, phi, None)
    for copy in band_copies:
        copy.wait_recv()
    s_low = products(table, 0, 6, phi, None, bl)
    s_up = products(table, 9, 6, phi, None, bu)
    to_pieces(part, jnp.concatenate([s_low, s_own, s_up], axis=1))

    rs_copies = []
    for k in range(1, n):
        col = up(c, k)
        copy = remote(part.at[col], rs_buf.at[k - 1], rs_s.at[k - 1], rs_r.at[k - 1], s, col)
        copy.start()
        rs_copies.append(copy)
    for copy in halo:
        copy.wait_recv()
    first = jnp.where(c == 0, 1, 0)
    last = jnp.where(c == n - 1, 1, 0)
    for p in range(27):
        if p < 9:
            low = lo[p].astype(F32) * (1 - first).astype(F32)
        else:
            low = lo[p - 9 * first].astype(F32)
        if p >= 18:
            high = hi[p].astype(F32) * (1 - last).astype(F32)
        else:
            high = hi[p + 9 * last].astype(F32)
        hphi[9 * (p // 3) + 3 + p % 3] = (base[p] - 0.5 * (low + high)).astype(BF16)
    h_mid = products(table, 6, 3, hphi, phi, None)

    total = part[c]
    for k in range(1, n):
        rs_copies[k - 1].wait_recv()
        total = total + rs_buf[k - 1]
    piece[...] = total
    ag[c] = total
    ag_copies = []
    for k in range(1, n):
        copy = remote(piece, ag.at[c], ag_s.at[k - 1], ag_r.at[k - 1], s, up(c, k))
        copy.start()
        ag_copies.append(copy)
    h_low = products(table, 0, 6, hphi, phi, bl)
    for copy in kn_copies:
        copy.wait_recv()
    panel = split(jnp.concatenate([unpack(k0n[0]), k0[...], unpack(k0n[1])], axis=0))
    for copy in ag_copies:
        copy.wait_recv()
    from_pieces(ag, mrow)
    m_own = mrow[...]
    bblk[...] = pack(dot3(split(m_own), panel))
    b_copies = []
    for k in range(1, n):
        copy = remote(bblk, ball.at[s], b_s.at[k - 1], b_r.at[k - 1], up(s, k), c)
        copy.start()
        b_copies.append(copy)
    ball[s] = bblk[...]
    h_up = products(table, 9, 6, hphi, phi, bu)
    to_pieces(
        part_h,
        jnp.concatenate(
            [h_low[:, ROWS:], h_low[:, :ROWS] + h_mid + h_up[:, :ROWS], h_up[:, ROWS:]], axis=1
        ),
    )
    rh_copies = []
    for k in range(1, n):
        col = up(c, k)
        copy = remote(part_h.at[col], rs_buf_h.at[k - 1], rh_s.at[k - 1], rh_r.at[k - 1], s, col)
        copy.start()
        rh_copies.append(copy)
    inside = jnp.where(active, 1.0, 0.0).astype(F32)

    def block(matrix):
        left, mid, right = (matrix[:, ROWS * i : ROWS * (i + 1)] for i in range(3))
        return jnp.where(e == 0, left, jnp.where(e == 1, mid, right)) * inside

    out[0] = block(m_own)

    for copy in kr_copies:
        copy.wait_recv()
    k0cat = split(side_by_side(k0row, n))
    for copy in b_copies:
        copy.wait_recv()
    bcol = split(stacked(ball, n))
    y_own = dot3(k0cat, bcol)
    y1[...] = pack(y_own)
    y_sends = []
    for i in range(3):
        target = up(s, i - 1)
        wanted = target != c
        copy = remote(y1, y1all.at[c], y_s.at[i], y_r.at[c], s, target)
        y_sends.append((wanted, copy))

        @pl.when(wanted)
        def _():
            copy.start()

    m_sends = []
    for i, d in enumerate((-2, -1, 1, 2)):
        target = up(s, d)
        wanted = up(c - target, 1) < 3
        copy = remote(mrow, mall.at[2 - d], m_s.at[i], m_r.at[i], target, c)
        m_sends.append((wanted, copy))

        @pl.when(wanted)
        def _():
            copy.start()

    out[2] = jnp.zeros((ROWS, ROWS), F32)
    out[1] = jnp.zeros((ROWS, ROWS), F32)
    total_h = part_h[c]
    for k in range(1, n):
        rh_copies[k - 1].wait_recv()
        total_h = total_h + rs_buf_h[k - 1]
    piece_h[...] = total_h
    h_sends = []
    for i in range(3):
        target = up(s, i - 1)
        wanted = target != c
        copy = remote(piece_h, ag_h.at[c], ah_s.at[i], ah_r.at[c], s, target)
        h_sends.append((wanted, copy))

        @pl.when(wanted)
        def _():
            copy.start()


    @pl.when(active)
    def _():
        y1all[c] = y1[...]
        ag_h[c] = piece_h[...]
        for k in range(1, n):
            other = up(c, k)
            remote(y1, y1all.at[other], y_s.at[0], y_r.at[other], s, other).wait_recv()
        ycat = split(side_by_side(y1all, n))
        first = mask * (3.0 * y_own - 2.0 * dot3(ycat, bcol))
        k1[...] = pack(first)
        for i, (d, f) in enumerate(pairs):
            t, v = up(s, d), up(s, d + f - 1)

            @pl.when(jnp.logical_not((d == 0) & (v == c)))
            def _():
                remote(k1, k1all.at[(2 - d) * 3 + e], k_s.at[i], k_r.at[(2 - d) * 3 + e], t, v).start()

        k1all[6 + e] = k1[...]
        mall[2] = m_own
        for i, d in enumerate((-2, -1, 1, 2)):
            remote(mrow, mall.at[2 - d], m_s.at[i], m_r.at[i], up(s, d), c).wait_recv()
        for i, (d, f) in enumerate(pairs):
            t, v = up(s, d), up(s, d + f - 1)

            @pl.when(jnp.logical_not((d == 0) & (v == c)))
            def _():
                remote(k1, k1all.at[i], k_s.at[i], k_r.at[i], t, v).wait_recv()

        for k in range(1, n):
            other = up(c, k)
            remote(piece_h, ag_h.at[other], ah_s.at[0], ah_r.at[other], s, other).wait_recv()
        from_pieces(ag_h, hrow)
        out[1] = block(hrow[...])
        kb = {}
        mb = {}
        for r in range(5):
            mr = mall[r]
            for f in range(3):
                kb[r, r + f] = unpack(k1all[3 * r + f])
                mb[r, r + f] = mr[:, ROWS * f : ROWS * f + ROWS]
        zero = jnp.zeros((ROWS, ROWS), F32)

        def window(blocks, rows, cols):
            return jnp.concatenate(
                [jnp.concatenate([blocks.get((r, q), zero) for q in cols], axis=1) for r in rows], axis=0
            )

        k_window = window(kb, range(5), range(7))
        m_window = split(window(mb, range(5), range(7)))
        x2 = dot3(split(window(kb, [2], [2, 3, 4])), split(window(mb, [1, 2, 3], range(1, 6))))
        y2 = dot3(split(x2), split(k_window))
        w2 = dot3(split(y2), m_window, (((1,), (1,)), ((), ())))
        columns = [
            jnp.concatenate([kb.get((r, q), zero) for r in range(5)], axis=0) for q in (2, 3, 4)
        ]
        kcol = jnp.where(e == 0, columns[0], jnp.where(e == 1, columns[1], columns[2]))
        y2s = jnp.where(
            e == 0, y2[:, 2 * ROWS : 3 * ROWS], jnp.where(e == 1, y2[:, 3 * ROWS : 4 * ROWS], y2[:, 4 * ROWS : 5 * ROWS])
        )
        out[2] = mask * (3.0 * y2s - 2.0 * dot3(split(w2), split(kcol)))
        for i, (d, f) in enumerate(pairs):
            t, v = up(s, d), up(s, d + f - 1)

            @pl.when(jnp.logical_not((d == 0) & (v == c)))
            def _():
                remote(k1, k1all.at[(2 - d) * 3 + e], k_s.at[i], k_r.at[i], t, v).wait_send()

    for copy in halo + band_copies + rs_copies + rh_copies + kn_copies + kr_copies + ag_copies + b_copies:
        copy.wait_send()
    for wanted, copy in m_sends + y_sends + h_sends:

        @pl.when(wanted)
        def _():
            copy.wait_send()


def slab_program(n, table, x, v, kernel, near):
    vmem = pl.BlockSpec(memory_space=pltpu.VMEM)
    dma = pltpu.SemaphoreType.DMA
    blocks = lambda count, rows=ROWS, kind=BF16: pltpu.VMEM((count, rows, 256), kind)
    half = lambda *lead: pltpu.VMEM((*lead, ROWS // 2, 2 * ROWS), F32)
    return pl.pallas_call(
        functools.partial(slab_kernel, n),
        out_shape=jax.ShapeDtypeStruct((3, ROWS, ROWS), F32),
        in_specs=[
            pl.BlockSpec(memory_space=pltpu.SMEM),
            vmem,
            pl.BlockSpec(memory_space=pl.ANY),
            vmem,
            vmem,
        ],
        out_specs=vmem,
        scratch_shapes=[
            blocks(90),
            blocks(90),
            blocks(63),
            blocks(63),
            blocks(27),
            blocks(27),
            blocks(27, kind=F32),
            blocks(27, ATOMS),
            pltpu.VMEM((n, 8, 2 * ROWS), F32),
            half(),
            pltpu.VMEM((n - 1, 8, 2 * ROWS), F32),
            pltpu.VMEM((8, 2 * ROWS), F32),
            pltpu.VMEM((n, 8, 2 * ROWS), F32),
            pltpu.VMEM((n, 8, 2 * ROWS), F32),
            pltpu.VMEM((n - 1, 8, 2 * ROWS), F32),
            pltpu.VMEM((8, 2 * ROWS), F32),
            pltpu.VMEM((n, 8, 2 * ROWS), F32),
            pltpu.VMEM((ROWS, 3 * ROWS), F32),
            half(n),
            half(2),
            half(),
            half(n),
            half(),
            half(n),
            half(),
            half(15),
            pltpu.VMEM((ROWS, 3 * ROWS), F32),
            pltpu.VMEM((5, ROWS, 3 * ROWS), F32),
            dma, dma((12,)), dma((12,)), dma((2,)), dma((2,)),
            pltpu.SemaphoreType.REGULAR((6,)),
            dma((n,)), dma((n,)), dma((n,)), dma((n,)), dma((n,)), dma((n,)), dma((3,)), dma((n,)),
            dma((n,)), dma((n,)),
            dma((2,)), dma((2,)), dma((n,)), dma((n,)), dma((3,)), dma((n,)),
            dma((15,)), dma((15,)), dma((4,)), dma((4,)),
        ],
        compiler_params=pltpu.CompilerParams(
            collective_id=0, has_side_effects=True, vmem_limit_bytes=40 * 1024 * 1024
        ),
    )(table, x, v, kernel, near)


def run_table(band, slab):
    cells = jnp.arange(30, dtype=jnp.int32)
    place = jnp.stack([cells // 6 + 3 * slab, cells % 6], axis=-1)
    offset = place[:, None, :] - band[None, :, :2]
    inside = jnp.all((offset >= 0) & (offset <= 2), axis=-1)
    start = (offset[..., 0] * 3 + offset[..., 1]) * 9 + 3 - band[None, :, 2]
    own = jnp.where(inside, start, 81)[:, ATOMS : 2 * ATOMS]
    lower = jnp.where(inside, start - 27, 54)[:, :ATOMS]
    upper = jnp.where(inside, start, 54)[:, 2 * ATOMS :]
    other = jnp.where(cells[:, None] < 12, lower, jnp.where(cells[:, None] < 18, 54, upper))
    return jnp.concatenate([own, other], axis=1).reshape(15, 64)


def local(supports, potential, anchors, kernel):
    slab = lax.axis_index("atoms")
    col = lax.axis_index("cols")
    x = supports.transpose(2, 3, 0, 1, 4).reshape(27, ROWS, 256)
    v = potential.transpose(1, 2, 0, 3).reshape(27, ATOMS, 256)
    far = jnp.full((ATOMS, 3), -100, jnp.int32)
    padded = jnp.concatenate([far, anchors, -2 * far], axis=0)
    band = lax.dynamic_slice_in_dim(padded, slab * ATOMS, 3 * ATOMS, 0)
    table = run_table(band, slab)
    rows = lax.dynamic_slice_in_dim(anchors, slab * ATOMS, ATOMS, 0)
    columns = lax.dynamic_slice_in_dim(anchors, col * ATOMS, ATOMS, 0)
    near = jnp.all(jnp.abs(columns[None] - rows[:, None]) <= 2, axis=-1).astype(F32)
    out = slab_program(lax.axis_size("atoms"), table, x, v, kernel, near)
    return out[0], out[1], out[2]


def solution(mesh):
    in_specs = (
        P("atoms", None, None, "cols", None),
        P("atoms", None, "cols", None),
        P(),
        P("atoms", "cols"),
    )
    out_specs = (P("atoms", "cols"), P("atoms", "cols"), P("atoms", "cols"))
    return jax.shard_map(local, mesh=mesh, in_specs=in_specs, out_specs=out_specs, check_vma=False)
```

```python
import functools

import jax
import jax.numpy as jnp
from jax import lax
from jax.experimental import pallas as pl
from jax.experimental.pallas import tpu as pltpu
from jax.sharding import PartitionSpec as P

MESH = pl.DeviceIdType.MESH
F32 = jnp.float32
BF16 = jnp.bfloat16
ATOMS = 16
FUNCS = 4
ROWS = ATOMS * FUNCS


def split(a):
    high = a.astype(BF16)
    return high, (a - high.astype(F32)).astype(BF16)


def dot3(left, right, dims=(((1,), (0,)), ((), ()))):
    lh, ll = left
    rh, rl = right
    mm = functools.partial(lax.dot_general, dimension_numbers=dims, preferred_element_type=F32)
    return mm(lh, rh) + (mm(lh, rl) + mm(ll, rh))


def shift_matrices():
    source = lax.broadcasted_iota(jnp.int32, (256, 256), 0)
    target = lax.broadcasted_iota(jnp.int32, (256, 256), 1)
    step = target - source
    z = target % 16
    one = jnp.float32(1.0)
    own = jnp.where(step == 0, -6.0, 0.0)
    own = own + jnp.where((step == 1) & (z != 0), one, 0.0)
    own = own + jnp.where((step == -1) & (z != 15), one, 0.0)
    own = own + jnp.where((step == 16) | (step == -16), one, 0.0)
    z_low = jnp.where((step == -15) & (z == 0), one, 0.0)
    z_high = jnp.where((step == 15) & (z == 15), one, 0.0)
    y_low = jnp.where(step == -240, one, 0.0)
    y_high = jnp.where(step == 240, one, 0.0)
    return [m.astype(BF16) for m in (own, z_low, z_high, y_low, y_high)]


def mm(a, b):
    return jnp.dot(a, b, preferred_element_type=F32)


def remote(src, dst, ss, rs, row, col):
    return pltpu.make_async_remote_copy(
        src_ref=src, dst_ref=dst, send_sem=ss, recv_sem=rs, device_id=(row, col), device_id_type=MESH
    )


def signal_barrier(row, col):
    pl.semaphore_signal(
        pltpu.get_barrier_semaphore(), inc=1, device_id=(row, col), device_id_type=MESH
    )


def pack(block):
    return jnp.concatenate([block[: ROWS // 2], block[ROWS // 2 :]], axis=1)


def unpack(packed):
    return jnp.concatenate([packed[:, :ROWS], packed[:, ROWS:]], axis=0)


def side_by_side(ref, n):
    lane = lax.broadcasted_iota(jnp.int32, (ROWS // 2, 2 * ROWS), 1) < ROWS
    tiles = []
    for t in range(0, n, 2):
        even, odd = ref[t], ref[t + 1]
        top = jnp.where(lane, even, pltpu.roll(odd, ROWS, 1))
        low = jnp.where(lane, pltpu.roll(even, ROWS, 1), odd)
        tiles.append(jnp.concatenate([top, low], axis=0))
    return jnp.concatenate(tiles, axis=1)


def stacked(ref, n):
    return jnp.concatenate([unpack(ref[t]) for t in range(n)], axis=0)


def gather(table, row, ref, at, shift):
    runs = [ref.at[pl.ds(table[at, shift + a], 6)] for a in range(ATOMS)]

    def block(z):
        tiles = []
        for i in range(4):
            rows = slice(16 * i, 16 * i + 16)
            picked = [runs[4 * i + j][z, rows, :] for j in range(4)]
            tiles.append(
                jnp.where(
                    row < 8,
                    jnp.where(row < 4, picked[0], picked[1]),
                    jnp.where(row < 12, picked[2], picked[3]),
                )
            )
        return jnp.concatenate(tiles, axis=0)

    return block


def products(table, start, count, left, own, band):
    row = lax.broadcasted_iota(jnp.int32, (16, 256), 0).astype(F32).astype(BF16)
    columns = ROWS * ((own is not None) + (band is not None))

    def step(i, acc):
        lefts, rights = [], []
        for k in range(2):
            at = start + i
            left_of = gather(table, row, left, at, 32 * k)
            own_of = None if own is None or own is left else gather(table, row, own, at, 32 * k)
            band_of = None if band is None else gather(table, row, band, at, 32 * k + 16)
            for z in range(6):
                first = left_of(z)
                lefts.append(first)
                parts = []
                if own is not None:
                    parts.append(first if own is left else own_of(z))
                if band is not None:
                    parts.append(band_of(z))
                rights.append(jnp.concatenate(parts, axis=0))
        return acc + lax.dot_general(
            jnp.concatenate(lefts, axis=1),
            jnp.concatenate(rights, axis=1),
            (((1,), (1,)), ((), ())),
            preferred_element_type=F32,
        )

    return lax.fori_loop(0, count, step, jnp.zeros((ROWS, columns), F32))


def to_pieces(ref, matrix):
    for a in range(ATOMS):
        ref[a, 0:4, :] = matrix[4 * a : 4 * a + 4, : 2 * ROWS]
        ref[a, 4:8, 0:ROWS] = matrix[4 * a : 4 * a + 4, 2 * ROWS :]
        ref[a, 4:8, ROWS:] = jnp.zeros((4, ROWS), F32)


def from_pieces(ref, rows):
    for a in range(ATOMS):
        rows[4 * a : 4 * a + 4, 0 : 2 * ROWS] = ref[a, 0:4, :]
        rows[4 * a : 4 * a + 4, 2 * ROWS :] = ref[a, 4:8, 0:ROWS]


def slab_kernel(
    n, table, x_ref, v_hbm, k0, near, out,
    phi, hphi, bl, bu, lo, hi, base, v_ref,
    part, k0p, rs_buf, piece, ag, part_h, rs_buf_h, piece_h, ag_h, hrow, k0row, k0n, bblk, ball, y1, y1all, k1, k1all, mrow, mall,
    v_sem, band_s, band_r, halo_s, halo_r, known,
    rs_s, rs_r, ag_s, ag_r, rh_s, rh_r, ah_s, ah_r, kr_s, kr_r, kn_s, kn_r, b_s, b_r, y_s, y_r, k_s, k_r, m_s, m_r,
):
    s = lax.axis_index("atoms")
    c = lax.axis_index("cols")
    up = lambda at, k: lax.rem(at + k + 2 * n, n)
    e = up(c - s, 1)
    active = e < 3
    pairs = [(d, f) for d in range(-2, 3) for f in range(3)]
    load = pltpu.make_async_copy(v_hbm, v_ref, v_sem)
    load.start()
    for d in (1, -1):
        signal_barrier(s, up(c, d))
        signal_barrier(up(s, d), c)
    k0p[...] = pack(k0[...])
    pl.semaphore_wait(pltpu.get_barrier_semaphore(), 4)

    def tell(step):
        for d in (1 << step, -(1 << step)):
            pl.semaphore_signal(known.at[step], inc=1, device_id=(s, up(c, d)), device_id_type=MESH)
            pl.semaphore_signal(known.at[3 + step], inc=1, device_id=(up(s, d), c), device_id_type=MESH)

    def learn(step):
        pl.semaphore_wait(known.at[step], 2)
        pl.semaphore_wait(known.at[3 + step], 2)

    tell(0)
    kn_copies = []
    for i, d in enumerate((1, -1)):
        copy = remote(k0p, k0n.at[i], kn_s.at[i], kn_r.at[i], up(s, d), c)
        copy.start()
        kn_copies.append(copy)
    halo = []
    band_copies = []

    def bulk(part_of):
        at = 9 * part_of
        copies = [
            remote(x_ref.at[at : at + 9], lo.at[at : at + 9], halo_s.at[part_of], halo_r.at[part_of], s, up(c, 1)),
            remote(
                x_ref.at[at : at + 9], hi.at[at : at + 9], halo_s.at[3 + part_of], halo_r.at[3 + part_of], s, up(c, -1)
            ),
        ]
        halo.extend(copies)
        for k in (2 * part_of, 2 * part_of + 1):
            source, target = x_ref.at[9 + 3 * k : 12 + 3 * k], bl.at[9 * k + 3 : 9 * k + 6]
            down = remote(source, target, band_s.at[k], band_r.at[k], up(s, 1), c)
            source, target = x_ref.at[3 * k : 3 * k + 3], bu.at[9 * k + 3 : 9 * k + 6]
            copies.extend([down, remote(source, target, band_s.at[6 + k], band_r.at[6 + k], up(s, -1), c)])
        band_copies.extend(copies[2:])
        for copy in copies:
            copy.start()

    bulk(0)
    learn(0)
    tell(1)
    bulk(1)
    own, z_low, z_high, y_low, y_high = shift_matrices()
    for bx in range(3):
        first = 9 * bx
        rows = lambda at, count: x_ref[first + at : first + at + count].reshape(count * ROWS, 256)
        base[first : first + 9] = mm(rows(0, 9), own).reshape(9, ROWS, 256)
        for by in range(3):
            f = 3 * by
            base[first + f + 1 : first + f + 3] += mm(rows(f, 2), z_low).reshape(2, ROWS, 256)
            base[first + f : first + f + 2] += mm(rows(f + 1, 2), z_high).reshape(2, ROWS, 256)
        base[first + 3 : first + 9] += mm(rows(0, 6), y_low).reshape(6, ROWS, 256)
        base[first : first + 6] += mm(rows(3, 6), y_high).reshape(6, ROWS, 256)
    learn(1)
    tell(2)
    bulk(2)
    spread = (
        lax.broadcasted_iota(jnp.int32, (ROWS, ATOMS), 0) // FUNCS
        == lax.broadcasted_iota(jnp.int32, (ROWS, ATOMS), 1)
    ).astype(F32).astype(BF16)
    load.wait()
    for p in range(27):
        base[p] = -0.5 * base[p] + mm(spread, v_ref[p]) * x_ref[p].astype(F32)
    for p in range(27):
        phi[9 * (p // 3) + 3 + p % 3] = x_ref[p]
    for ref in (phi, hphi):
        for at in range(0, 81, 9):
            ref[at : at + 3] = jnp.zeros((3, ROWS, 256), BF16)
            ref[at + 6 : at + 9] = jnp.zeros((3, ROWS, 256), BF16)
        ref[81:90] = jnp.zeros((9, ROWS, 256), BF16)
    for ref in (bl, bu):
        for at in range(0, 54, 9):
            ref[at : at + 3] = jnp.zeros((3, ROWS, 256), BF16)
            ref[at + 6 : at + 9] = jnp.zeros((3, ROWS, 256), BF16)
        ref[54:63] = jnp.zeros((9, ROWS, 256), BF16)
    mask = lax.dot_general(
        mm(spread, near[...].astype(BF16)).astype(BF16),
        spread,
        (((1,), (1,)), ((), ())),
        preferred_element_type=F32,
    )
    learn(2)
    kr_copies = []
    for k in range(1, n):
        copy = remote(k0p, k0row.at[c], kr_s.at[k - 1], kr_r.at[k - 1], s, up(c, k))
        copy.start()
        kr_copies.append(copy)
    k0row[c] = k0p[...]
    s_own = products(table, 0, 15, phi, phi, None)
    for copy in band_copies:
        copy.wait_recv()
    s_low = products(table, 0, 6, phi, None, bl)
    s_up = products(table, 9, 6, phi, None, bu)
    to_pieces(part, jnp.concatenate([s_low, s_own, s_up], axis=1))

    rs_copies = []
    for k in range(1, n):
        col = up(c, k)
        copy = remote(part.at[col], rs_buf.at[k - 1], rs_s.at[k - 1], rs_r.at[k - 1], s, col)
        copy.start()
        rs_copies.append(copy)
    for copy in halo:
        copy.wait_recv()
    first = jnp.where(c == 0, 1, 0)
    last = jnp.where(c == n - 1, 1, 0)
    for p in range(27):
        if p < 9:
            low = lo[p].astype(F32) * (1 - first).astype(F32)
        else:
            low = lo[p - 9 * first].astype(F32)
        if p >= 18:
            high = hi[p].astype(F32) * (1 - last).astype(F32)
        else:
            high = hi[p + 9 * last].astype(F32)
        hphi[9 * (p // 3) + 3 + p % 3] = (base[p] - 0.5 * (low + high)).astype(BF16)
    h_mid = products(table, 6, 3, hphi, phi, None)

    total = part[c]
    for k in range(1, n):
        rs_copies[k - 1].wait_recv()
        total = total + rs_buf[k - 1]
    piece[...] = total
    ag[c] = total
    ag_copies = []
    for k in range(1, n):
        copy = remote(piece, ag.at[c], ag_s.at[k - 1], ag_r.at[k - 1], s, up(c, k))
        copy.start()
        ag_copies.append(copy)
    h_low = products(table, 0, 6, hphi, phi, bl)
    for copy in kn_copies:
        copy.wait_recv()
    panel = split(jnp.concatenate([unpack(k0n[0]), k0[...], unpack(k0n[1])], axis=0))
    for copy in ag_copies:
        copy.wait_recv()
    from_pieces(ag, mrow)
    m_own = mrow[...]
    bblk[...] = pack(dot3(split(m_own), panel))
    b_copies = []
    for k in range(1, n):
        copy = remote(bblk, ball.at[s], b_s.at[k - 1], b_r.at[k - 1], up(s, k), c)
        copy.start()
        b_copies.append(copy)
    ball[s] = bblk[...]
    inside = jnp.where(active, 1.0, 0.0).astype(F32)

    def block(matrix):
        left, mid, right = (matrix[:, ROWS * i : ROWS * (i + 1)] for i in range(3))
        return jnp.where(e == 0, left, jnp.where(e == 1, mid, right)) * inside

    out[0] = block(m_own)

    for copy in kr_copies:
        copy.wait_recv()
    k0cat = split(side_by_side(k0row, n))
    for copy in b_copies:
        copy.wait_recv()
    bcol = split(stacked(ball, n))
    y_own = dot3(k0cat, bcol)
    y1[...] = pack(y_own)
    y_sends = []
    for i in range(3):
        target = up(s, i - 1)
        wanted = target != c
        copy = remote(y1, y1all.at[c], y_s.at[i], y_r.at[c], s, target)
        y_sends.append((wanted, copy))

        @pl.when(wanted)
        def _():
            copy.start()

    m_sends = []
    for i, d in enumerate((-2, -1, 1, 2)):
        target = up(s, d)
        wanted = up(c - target, 1) < 3
        copy = remote(mrow, mall.at[2 - d], m_s.at[i], m_r.at[i], target, c)
        m_sends.append((wanted, copy))

        @pl.when(wanted)
        def _():
            copy.start()

    out[2] = jnp.zeros((ROWS, ROWS), F32)
    out[1] = jnp.zeros((ROWS, ROWS), F32)
    h_up = products(table, 9, 6, hphi, phi, bu)
    to_pieces(
        part_h,
        jnp.concatenate(
            [h_low[:, ROWS:], h_low[:, :ROWS] + h_mid + h_up[:, :ROWS], h_up[:, ROWS:]], axis=1
        ),
    )
    rh_copies = []
    for k in range(1, n):
        col = up(c, k)
        copy = remote(part_h.at[col], rs_buf_h.at[k - 1], rh_s.at[k - 1], rh_r.at[k - 1], s, col)
        copy.start()
        rh_copies.append(copy)

    @pl.when(active)
    def _():
        y1all[c] = y1[...]
        for k in range(1, n):
            other = up(c, k)
            remote(y1, y1all.at[other], y_s.at[0], y_r.at[other], s, other).wait_recv()
        ycat = split(side_by_side(y1all, n))
        first = mask * (3.0 * y_own - 2.0 * dot3(ycat, bcol))
        k1[...] = pack(first)
        for i, (d, f) in enumerate(pairs):
            t, v = up(s, d), up(s, d + f - 1)

            @pl.when(jnp.logical_not((d == 0) & (v == c)))
            def _():
                remote(k1, k1all.at[(2 - d) * 3 + e], k_s.at[i], k_r.at[(2 - d) * 3 + e], t, v).start()

        k1all[6 + e] = k1[...]

    total_h = part_h[c]
    for k in range(1, n):
        rh_copies[k - 1].wait_recv()
        total_h = total_h + rs_buf_h[k - 1]
    piece_h[...] = total_h
    h_sends = []
    for i in range(3):
        target = up(s, i - 1)
        wanted = target != c
        copy = remote(piece_h, ag_h.at[c], ah_s.at[i], ah_r.at[c], s, target)
        h_sends.append((wanted, copy))

        @pl.when(wanted)
        def _():
            copy.start()

    @pl.when(active)
    def _():
        ag_h[c] = piece_h[...]
        mall[2] = m_own
        for i, d in enumerate((-2, -1, 1, 2)):
            remote(mrow, mall.at[2 - d], m_s.at[i], m_r.at[i], up(s, d), c).wait_recv()
        for i, (d, f) in enumerate(pairs):
            t, v = up(s, d), up(s, d + f - 1)

            @pl.when(jnp.logical_not((d == 0) & (v == c)))
            def _():
                remote(k1, k1all.at[i], k_s.at[i], k_r.at[i], t, v).wait_recv()

        kb = {}
        mb = {}
        for r in range(5):
            mr = mall[r]
            for f in range(3):
                kb[r, r + f] = unpack(k1all[3 * r + f])
                mb[r, r + f] = mr[:, ROWS * f : ROWS * f + ROWS]
        zero = jnp.zeros((ROWS, ROWS), F32)

        def window(blocks, rows, cols):
            return jnp.concatenate(
                [jnp.concatenate([blocks.get((r, q), zero) for q in cols], axis=1) for r in rows], axis=0
            )

        k_window = window(kb, range(5), range(7))
        m_window = split(window(mb, range(5), range(7)))
        x2 = dot3(split(window(kb, [2], [2, 3, 4])), split(window(mb, [1, 2, 3], range(1, 6))))
        y2 = dot3(split(x2), split(k_window))
        w2 = dot3(split(y2), m_window, (((1,), (1,)), ((), ())))
        columns = [
            jnp.concatenate([kb.get((r, q), zero) for r in range(5)], axis=0) for q in (2, 3, 4)
        ]
        kcol = jnp.where(e == 0, columns[0], jnp.where(e == 1, columns[1], columns[2]))
        y2s = jnp.where(
            e == 0, y2[:, 2 * ROWS : 3 * ROWS], jnp.where(e == 1, y2[:, 3 * ROWS : 4 * ROWS], y2[:, 4 * ROWS : 5 * ROWS])
        )
        out[2] = mask * (3.0 * y2s - 2.0 * dot3(split(w2), split(kcol)))
        for k in range(1, n):
            other = up(c, k)
            remote(piece_h, ag_h.at[other], ah_s.at[0], ah_r.at[other], s, other).wait_recv()
        from_pieces(ag_h, hrow)
        out[1] = block(hrow[...])
        for i, (d, f) in enumerate(pairs):
            t, v = up(s, d), up(s, d + f - 1)

            @pl.when(jnp.logical_not((d == 0) & (v == c)))
            def _():
                remote(k1, k1all.at[(2 - d) * 3 + e], k_s.at[i], k_r.at[i], t, v).wait_send()

    for copy in halo + band_copies + rs_copies + rh_copies + kn_copies + kr_copies + ag_copies + b_copies:
        copy.wait_send()
    for wanted, copy in m_sends + y_sends + h_sends:

        @pl.when(wanted)
        def _():
            copy.wait_send()


def slab_program(n, table, x, v, kernel, near):
    vmem = pl.BlockSpec(memory_space=pltpu.VMEM)
    dma = pltpu.SemaphoreType.DMA
    blocks = lambda count, rows=ROWS, kind=BF16: pltpu.VMEM((count, rows, 256), kind)
    half = lambda *lead: pltpu.VMEM((*lead, ROWS // 2, 2 * ROWS), F32)
    return pl.pallas_call(
        functools.partial(slab_kernel, n),
        out_shape=jax.ShapeDtypeStruct((3, ROWS, ROWS), F32),
        in_specs=[
            pl.BlockSpec(memory_space=pltpu.SMEM),
            vmem,
            pl.BlockSpec(memory_space=pl.ANY),
            vmem,
            vmem,
        ],
        out_specs=vmem,
        scratch_shapes=[
            blocks(90),
            blocks(90),
            blocks(63),
            blocks(63),
            blocks(27),
            blocks(27),
            blocks(27, kind=F32),
            blocks(27, ATOMS),
            pltpu.VMEM((n, 8, 2 * ROWS), F32),
            half(),
            pltpu.VMEM((n - 1, 8, 2 * ROWS), F32),
            pltpu.VMEM((8, 2 * ROWS), F32),
            pltpu.VMEM((n, 8, 2 * ROWS), F32),
            pltpu.VMEM((n, 8, 2 * ROWS), F32),
            pltpu.VMEM((n - 1, 8, 2 * ROWS), F32),
            pltpu.VMEM((8, 2 * ROWS), F32),
            pltpu.VMEM((n, 8, 2 * ROWS), F32),
            pltpu.VMEM((ROWS, 3 * ROWS), F32),
            half(n),
            half(2),
            half(),
            half(n),
            half(),
            half(n),
            half(),
            half(15),
            pltpu.VMEM((ROWS, 3 * ROWS), F32),
            pltpu.VMEM((5, ROWS, 3 * ROWS), F32),
            dma, dma((12,)), dma((12,)), dma((6,)), dma((6,)),
            pltpu.SemaphoreType.REGULAR((6,)),
            dma((n,)), dma((n,)), dma((n,)), dma((n,)), dma((n,)), dma((n,)), dma((3,)), dma((n,)),
            dma((n,)), dma((n,)),
            dma((2,)), dma((2,)), dma((n,)), dma((n,)), dma((3,)), dma((n,)),
            dma((15,)), dma((15,)), dma((4,)), dma((4,)),
        ],
        compiler_params=pltpu.CompilerParams(
            collective_id=0, has_side_effects=True, vmem_limit_bytes=40 * 1024 * 1024
        ),
    )(table, x, v, kernel, near)


def run_table(band, slab):
    cells = jnp.arange(30, dtype=jnp.int32)
    place = jnp.stack([cells // 6 + 3 * slab, cells % 6], axis=-1)
    offset = place[:, None, :] - band[None, :, :2]
    inside = jnp.all((offset >= 0) & (offset <= 2), axis=-1)
    start = (offset[..., 0] * 3 + offset[..., 1]) * 9 + 3 - band[None, :, 2]
    own = jnp.where(inside, start, 81)[:, ATOMS : 2 * ATOMS]
    lower = jnp.where(inside, start - 27, 54)[:, :ATOMS]
    upper = jnp.where(inside, start, 54)[:, 2 * ATOMS :]
    other = jnp.where(cells[:, None] < 12, lower, jnp.where(cells[:, None] < 18, 54, upper))
    return jnp.concatenate([own, other], axis=1).reshape(15, 64)


def local(supports, potential, anchors, kernel):
    slab = lax.axis_index("atoms")
    col = lax.axis_index("cols")
    x = supports.transpose(2, 3, 0, 1, 4).reshape(27, ROWS, 256)
    v = potential.transpose(1, 2, 0, 3).reshape(27, ATOMS, 256)
    far = jnp.full((ATOMS, 3), -100, jnp.int32)
    padded = jnp.concatenate([far, anchors, -2 * far], axis=0)
    band = lax.dynamic_slice_in_dim(padded, slab * ATOMS, 3 * ATOMS, 0)
    table = run_table(band, slab)
    rows = lax.dynamic_slice_in_dim(anchors, slab * ATOMS, ATOMS, 0)
    columns = lax.dynamic_slice_in_dim(anchors, col * ATOMS, ATOMS, 0)
    near = jnp.all(jnp.abs(columns[None] - rows[:, None]) <= 2, axis=-1).astype(F32)
    out = slab_program(lax.axis_size("atoms"), table, x, v, kernel, near)
    return out[0], out[1], out[2]


def solution(mesh):
    in_specs = (
        P("atoms", None, None, "cols", None),
        P("atoms", None, "cols", None),
        P(),
        P("atoms", "cols"),
    )
    out_specs = (P("atoms", "cols"), P("atoms", "cols"), P("atoms", "cols"))
    return jax.shard_map(local, mesh=mesh, in_specs=in_specs, out_specs=out_specs, check_vma=False)
```
